128 devices in a mesh: gx: 32 (over z, y, core), gy: 4 (over x).
Axes of the slice: x: 4, y: 4, z: 4, core: 2. Of those that a mesh axis runs over, the one named last changes fastest.
Arguments:
- tokens: bfloat16 [512, 9216], P(('gx', 'gy')), may hold values from -6 to 6
- gain: float32 [9216], replicated, may hold values from 0.1 to 1.9
- w_gate: bfloat16 [9216, 36864], P('gy', 'gx'), may hold values from -0.0625 to 0.0625
- w_up: bfloat16 [9216, 36864], P('gy', 'gx'), may hold values from -0.0625 to 0.0625
- w_down: bfloat16 [36864, 9216], P('gx', 'gy'), may hold values from -0.03125 to 0.03125
- w_kv: bfloat16 [4, 2304, 512], P('gy', 'gx'), may hold values from -0.0625 to 0.0625
- queries: bfloat16 [512, 12288], P(('gx', 'gy')), may hold values from -64 to 64
- key_cache: bfloat16 [512, 2048, 256], P(('gx', 'gy')), may hold values from -4 to 4
- value_cache: bfloat16 [512, 2048, 256], P(('gx', 'gy')), may hold values from -6 to 6
- lengths: int32 [512], P(('gx', 'gy')), may hold values from 2 to 2048, as said below
Outputs:
- mixed: bfloat16 [512, 9216], P(('gx', 'gy'))
- context: bfloat16 [512, 12288], P(('gx', 'gy'))
The draws below stay inside these ranges and needn't reach their ends.
Inputs may be any that keep to these rules, and one draw needn't show every extreme that they name: `lengths`: each row has at least two live slots, and some row fills all 2048 slots.
All inputs are finite; a program needn't handle non-finite values.
Results may differ from the reference program's by a relative error of at most 0.0055.
Values may be sent and summed in bfloat16 or wider, within the bound.
A program may use at most 128 MiB of HBM per device.

```python
import jax
import jax.numpy as jnp
from jax import lax

D = 9216
FF = 36864
HEADS = 48
HD = 256
CTX = 2048
ROWS = 512
N_GY = 4


def cache_keys(key):
    return jnp.clip(jax.random.normal(jax.random.fold_in(key, 11), (ROWS, CTX, HD), jnp.float32), -4.0, 4.0)


def draw_key_cache(key, part):
    keys = cache_keys(key)
    return keys.astype(jnp.bfloat16)


def draw_queries(key, part):
    drawn = jnp.clip(jax.random.normal(jax.random.fold_in(key, 15), (ROWS, HEADS, HD), jnp.float32), -4.0, 4.0)
    return drawn.reshape(ROWS, HEADS * HD).astype(jnp.bfloat16)


def draw_lengths(key, part):
    base = jax.random.randint(jax.random.fold_in(key, 17), (ROWS,), 2, CTX + 1)
    filled = jax.random.randint(jax.random.fold_in(key, 18), (), 0, ROWS)
    return jnp.where(jnp.arange(ROWS) == filled, CTX, base).astype(jnp.int32)


def block_scale(own_key, shape, pieces, low, top_value):
    level = 1.0
    for axis_at, shards_of in pieces:
        heights = jax.random.uniform(jax.random.fold_in(jax.random.fold_in(own_key, 6), axis_at), (shards_of,), jnp.float32, low / len(pieces), top_value / len(pieces))
        level = level * jnp.repeat(jnp.exp(heights), shape[axis_at] // shards_of).reshape((-1,) + (1,) * (len(shape) - 1 - axis_at))
    return level


def scatter_about(own_key, dims, scale, bound, cuts=(), dtype=jnp.bfloat16):
    loudness = block_scale(own_key, dims, cuts, -0.22, 0.18) if cuts else 1.0
    entries = jax.random.normal(own_key, dims, jnp.float32) * scale * loudness
    return jnp.minimum(jnp.maximum(entries, -bound), bound).astype(dtype)


def setup_inputs(seed: int = 0) -> dict:
    key_list = jax.random.split(jax.random.key(seed), 11)
    return {
        "tokens": scatter_about(key_list[0], (ROWS, D), 1.0, 6.0, ((0, 128),)),
        "gain": jnp.clip(1.0 + 0.18 * jax.random.normal(key_list[1], (D,), jnp.float32), 0.1, 1.9),
        "w_gate": scatter_about(key_list[2], (D, FF), D ** -0.5, 0.0625, ((0, 4), (1, 32))),
        "w_up": scatter_about(key_list[3], (D, FF), D ** -0.5, 0.0625, ((0, 4), (1, 32))),
        "w_down": scatter_about(key_list[4], (FF, D), FF ** -0.5, 0.03125, ((0, 32), (1, 4))),
        "w_kv": scatter_about(key_list[5], (N_GY, D // N_GY, 2 * HD), D ** -0.5, 0.0625, ((0, 4), (1, 32))),
        "queries": draw_queries(jax.random.fold_in(key_list[10], 71), 0),
        "key_cache": draw_key_cache(jax.random.fold_in(key_list[10], 71), 0),
        "value_cache": scatter_about(key_list[8], (ROWS, CTX, HD), 1.0, 6.0, ((0, 128),)),
        "lengths": draw_lengths(jax.random.fold_in(key_list[10], 71), 0),
    }


def layer_norm(tokens, gain):
    values = tokens.astype(jnp.float32)
    centred = values - lax.optimization_barrier(jnp.mean(values, axis=-1, keepdims=True))
    spread = lax.optimization_barrier(jnp.mean(centred * centred, axis=-1, keepdims=True))
    return (centred * lax.rsqrt(spread + 1e-05) * gain).astype(jnp.bfloat16)

def attend_row(inputs):
    query, keys, values, length, key_new, value_new = inputs
    grouped = query.reshape(HEADS, HD).astype(jnp.float32)
    scale = 1.0 / HD ** 0.5
    scores = jnp.dot(grouped, keys.astype(jnp.float32).T, preferred_element_type=jnp.float32) * scale
    own = jnp.dot(grouped, key_new.astype(jnp.float32), preferred_element_type=jnp.float32) * scale
    live = jnp.arange(CTX) < length
    scores = jnp.where(live[None, :], scores, -jnp.inf)
    top = jnp.maximum(lax.optimization_barrier(jnp.max(scores, axis=-1)), own)
    weights = jnp.exp(scores - top[:, None])
    own_weight = jnp.exp(own - top)
    total = lax.optimization_barrier(jnp.sum(weights, axis=-1)) + own_weight
    probs = (weights / total[:, None]).astype(jnp.bfloat16)
    own_prob = (own_weight / total).astype(jnp.bfloat16)
    context = jnp.dot(probs, values, preferred_element_type=jnp.float32)
    context = context + own_prob.astype(jnp.float32)[:, None] * value_new.astype(jnp.float32)[None, :]
    return context.reshape(-1).astype(jnp.bfloat16)

def reference(tokens, gain, w_gate, w_up, w_down, w_kv, queries, key_cache, value_cache, lengths):
    normed = layer_norm(tokens, gain)
    gate = jnp.dot(normed, w_gate, preferred_element_type=jnp.float32)
    up = jnp.dot(normed, w_up, preferred_element_type=jnp.float32)
    hidden = (jax.nn.silu(gate) * up).astype(jnp.bfloat16)
    ffn = jnp.dot(hidden, w_down, preferred_element_type=jnp.float32)
    mixed = (tokens.astype(jnp.float32) + ffn).astype(jnp.bfloat16)
    fresh = jnp.dot(normed, w_kv.reshape(D, 2 * HD), preferred_element_type=jnp.float32)
    key_new = fresh[:, :HD].astype(jnp.bfloat16)
    value_new = fresh[:, HD:].astype(jnp.bfloat16)
    context = lax.map(attend_row, (queries, key_cache, value_cache, lengths, key_new, value_new))
    return (mixed, context)
```

```python
import functools
import math

import jax
import jax.numpy as jnp
from jax import lax
from jax.experimental import pallas as pl
from jax.experimental.pallas import tpu as pltpu
from jax.sharding import PartitionSpec as P

MESH = pl.DeviceIdType.MESH
HD = 256
HEADS = 48
NZ, NY, NC, NX = 4, 4, 2, 4
SLAB = 16
TILE = 128
GRAN = 3
F32 = jnp.float32
BF16 = jnp.bfloat16


def step_kernel(
    tokens_ref, gain_ref, q_ref, len_ref, wkv_ref,
    wg_hbm, wu_hbm, wd_hbm, k_hbm, v_hbm,
    mixed_ref, ctx_ref,
    kbuf, vbuf, wgu, wd, nx, xr, xa, wpad, kp, kr, ks, kzr, kyr, kts, kt2r, kx, kxr,
    ps, rv, hs, dp, dr, ds_, azr, byr, ta, tb, tar, tbr, fx, fxr,
    m_s, l_s, acc_s, ssem, rsem, lsem,
):
    d_dev = xa.shape[-1]
    half = d_dev // 2
    gx = lax.axis_index("gx")
    x = lax.axis_index("gy")
    z = gx // (NY * NC)
    y = lax.rem(gx // NC, NY)
    c = lax.rem(gx, NC)
    oc = 1 - c

    def dev(dz=0, dy=0, dc=0, dx=0):
        zz, yy, cc = lax.rem(z + dz, NZ), lax.rem(y + dy, NY), lax.rem(c + dc, NC)
        return ((zz * NY + yy) * NC + cc, lax.rem(x + dx, NX))

    counter = [0]
    sent = []

    def rcopy(src, dst, device):
        i = counter[0]
        counter[0] += 1
        cp = pltpu.make_async_remote_copy(
            src_ref=src, dst_ref=dst, send_sem=ssem.at[i], recv_sem=rsem.at[i],
            device_id=device, device_id_type=MESH,
        )
        cp.start()
        sent.append(cp)
        return cp

    bar = pltpu.get_barrier_semaphore()
    peers = (
        [dev(dz=i) for i in range(1, NZ)] + [dev(dy=i) for i in range(1, NY)]
        + [dev(dx=i) for i in range(1, NX)] + [dev(dc=1)]
    )
    for peer in peers:
        pl.semaphore_signal(bar, inc=1, device_id=peer, device_id_type=MESH)

    kcp = [pltpu.make_async_copy(k_hbm.at[r], kbuf.at[r], lsem.at[0, r]) for r in range(4)]
    vcp = [pltpu.make_async_copy(v_hbm.at[r], vbuf.at[r], lsem.at[1, r]) for r in range(4)]
    for r in range(4):
        kcp[r].start()
        vcp[r].start()
    n_tiles = wgu.shape[0]

    def weight_copies(t):
        cols = pl.ds(pl.multiple_of(t * TILE, TILE), TILE)
        return (
            pltpu.make_async_copy(wg_hbm.at[:, cols], wgu.at[t, :, pl.ds(0, TILE)], lsem.at[2, t]),
            pltpu.make_async_copy(wu_hbm.at[:, cols], wgu.at[t, :, pl.ds(TILE, TILE)], lsem.at[3, t]),
        )

    for t in range(n_tiles):
        for cp in weight_copies(t):
            cp.start()
    wdcp = pltpu.make_async_copy(wd_hbm, wd, lsem.at[4, 0])
    wdcp.start()

    values = tokens_ref[...].astype(F32)
    centred = values - jnp.mean(values, axis=-1, keepdims=True)
    spread = jnp.mean(centred * centred, axis=-1, keepdims=True)
    normed = centred * lax.rsqrt(spread + 1e-05) * gain_ref[...]
    for j in range(NX):
        nx[j] = normed[:, j * d_dev : (j + 1) * d_dev]

    pl.semaphore_wait(bar, len(peers))

    cps = [
        rcopy(nx.at[lax.rem(x + i, NX)], xr.at[x], dev(dx=i)) for i in range(1, NX)
    ]
    xr[x] = nx[x]
    for cp in cps:
        cp.wait_recv()
    xa[c, z, y] = jnp.concatenate([xr[j] for j in range(NX)], axis=0).astype(BF16)

    ca, cb = pl.ds(0, half), pl.ds(half, half)
    st1 = [
        rcopy(xa.at[c, z, y, :, ca], xa.at[c, z, y, :, ca], dev(dy=i)) for i in range(1, NY)
    ] + [
        rcopy(xa.at[c, z, y, :, cb], xa.at[c, z, y, :, cb], dev(dz=i)) for i in range(1, NZ)
    ]

    scale = 1.0 / math.sqrt(HD)

    def attend(r):
        s = lax.dot_general(
            q_ref[r], kbuf[r], (((1,), (1,)), ((), ())), preferred_element_type=F32
        ) * scale
        live = lax.broadcasted_iota(jnp.int32, s.shape, 1) < len_ref[r]
        s = jnp.where(live, s, -jnp.inf)
        m = jnp.max(s, axis=-1, keepdims=True)
        p = jnp.exp(s - m)
        l = jnp.sum(p, axis=-1, keepdims=True)
        m_s[r] = jnp.broadcast_to(m, m_s.shape[1:])
        l_s[r] = jnp.broadcast_to(l, l_s.shape[1:])
        acc_s[r] = jnp.dot(p.astype(BF16), vbuf[r], preferred_element_type=F32)

    kcp[0].wait()
    vcp[0].wait()
    attend(0)

    for cp in st1:
        cp.wait_recv()
    st2 = [
        rcopy(xa.at[c, z, :, :, ca], xa.at[c, z, :, :, ca], dev(dz=i)) for i in range(1, NZ)
    ] + [
        rcopy(xa.at[c, :, y, :, cb], xa.at[c, :, y, :, cb], dev(dy=i)) for i in range(1, NY)
    ]
    for r in range(1, 4):
        kcp[r].wait()
        vcp[r].wait()
    lax.fori_loop(1, 4, lambda r, _: (attend(r), 0)[1], 0)

    span = wkv_ref.shape[0]
    offset = gx * span
    start = jnp.minimum(offset // TILE, d_dev // TILE - 2) * TILE
    wide = jnp.concatenate(
        [wkv_ref[...].astype(F32), jnp.zeros((2 * TILE - span, 2 * HD), F32)], axis=0
    )
    wpad[...] = pltpu.roll(wide, offset - start, axis=0).astype(BF16)

    for cp in st2:
        cp.wait_recv()
    sib = rcopy(xa.at[c], xa.at[c], dev(dc=1))
    sib.wait_recv()

    rows = NC * NZ * NY * SLAB

    def reduce_core(part, other, out, cols):
        def add(i, _):
            a, b = i // NY, lax.rem(i, NY)
            out[a, b] = (part[c, a, b].astype(F32) + other[a, b].astype(F32)).astype(out.dtype)
            return 0

        lax.fori_loop(0, NZ * NY, add, 0)

    def reduce_first(out, az, by, ha, hb):
        return [
            rcopy(out.at[lax.rem(z + i, NZ), :, :, ha], az.at[i - 1], dev(dz=i)) for i in range(1, NZ)
        ] + [
            rcopy(out.at[:, lax.rem(y + i, NY), :, hb], by.at[i - 1], dev(dy=i)) for i in range(1, NY)
        ]

    def reduce_second(out, az, by, ta, tb, tar, tbr, ha, hb):
        def add_a(b, _):
            total = out[z, b, :, ha].astype(F32)
            for i in range(NZ - 1):
                total += az[i, b].astype(F32)
            ta[b] = total.astype(ta.dtype)
            return 0

        def add_b(a, _):
            total = out[a, y, :, hb].astype(F32)
            for i in range(NY - 1):
                total += by[i, a].astype(F32)
            tb[a] = total.astype(tb.dtype)
            return 0

        lax.fori_loop(0, NY, add_a, 0)
        cps = [rcopy(ta.at[lax.rem(y + i, NY)], tar.at[i - 1], dev(dy=i)) for i in range(1, NY)]
        lax.fori_loop(0, NZ, add_b, 0)
        return cps + [rcopy(tb.at[lax.rem(z + i, NZ)], tbr.at[i - 1], dev(dz=i)) for i in range(1, NZ)]

    def reduce_last(ta, tb, tar, tbr):
        a, b = ta[y].astype(F32), tb[z].astype(F32)
        for i in range(NY - 1):
            a += tar[i].astype(F32)
        for i in range(NZ - 1):
            b += tbr[i].astype(F32)
        return a, b

    xwin = xa[:, :, :, :, pl.ds(pl.multiple_of(start, TILE), 2 * TILE)].reshape(rows, 2 * TILE)
    kp[...] = jnp.dot(xwin, wpad[...], preferred_element_type=F32).reshape(kp.shape)
    ka, kb = pl.ds(0, HD), pl.ds(HD, HD)
    kv_core = rcopy(kp.at[oc], kr, dev(dc=1))

    per = n_tiles // GRAN
    chunk = rows // NX

    def gate_up(g):
        def tile(t, _):
            col = pl.ds(pl.multiple_of(t * 2 * TILE, 2 * TILE), 2 * TILE)
            for cp in weight_copies(g * per + t):
                cp.wait()
            part = jnp.dot(
                xa[...].reshape(rows, d_dev), wgu[g * per + t], preferred_element_type=F32
            )
            for k in range(NX):
                ps[k, g, :, col] = part[k * chunk : (k + 1) * chunk].astype(BF16)
            return 0

        lax.fori_loop(0, per, tile, 0)
        return [
            rcopy(ps.at[lax.rem(x + i, NX), g], rv.at[i - 1, g], dev(dx=i)) for i in range(1, NX)
        ]

    def activate(g, cps):
        for cp in cps:
            cp.wait_recv()
        for t in range(per):
            col = pl.ds(t * 2 * TILE, 2 * TILE)
            total = ps[x, g, :, col].astype(F32)
            for i in range(NX - 1):
                total += rv[i, g, :, col].astype(F32)
            gate, up = total[:, :TILE], total[:, TILE:]
            hs[x, :, pl.ds((g * per + t) * TILE, TILE)] = (
                gate / (1.0 + jnp.exp(-gate)) * up
            ).astype(BF16)
        cols = pl.ds(g * per * TILE, per * TILE)
        return [rcopy(hs.at[x, :, cols], hs.at[x, :, cols], dev(dx=i)) for i in range(1, NX)]

    g0 = gate_up(0)
    kv_core.wait_recv()
    reduce_core(kp, kr, ks, 2 * HD)
    kv1 = reduce_first(ks, kzr, kyr, ka, kb)
    g1 = gate_up(1)
    for cp in kv1:
        cp.wait_recv()
    kv2 = reduce_second(
        ks, kzr, kyr, kts.at[0], kts.at[1], kt2r.at[0], kt2r.at[1], ka, kb
    )
    g2 = gate_up(2)
    for cp in kv2:
        cp.wait_recv()
    key_sum, value_sum = reduce_last(kts.at[0], kts.at[1], kt2r.at[0], kt2r.at[1])
    for j in range(NX):
        kx[j] = jnp.concatenate([key_sum[4 * j : 4 * j + 4], value_sum[4 * j : 4 * j + 4]], axis=1)
    kv3 = [rcopy(kx.at[lax.rem(x + i, NX)], kxr.at[i - 1], dev(dx=i)) for i in range(1, NX)]
    h0 = activate(0, g0)
    for cp in kv3:
        cp.wait_recv()
    fresh = kx[x]
    for i in range(NX - 1):
        fresh += kxr[i]
    fresh = fresh.astype(BF16).astype(F32)
    for r in range(4):
        key_new, value_new = fresh[r : r + 1, :HD], fresh[r : r + 1, HD:]
        s_new = jnp.sum(q_ref[r].astype(F32) * key_new, axis=-1, keepdims=True) * scale
        m_old = m_s[r][:, :1]
        m = jnp.maximum(m_old, s_new)
        keep, own = jnp.exp(m_old - m), jnp.exp(s_new - m)
        total = l_s[r][:, :1] * keep + own
        prob = (own / total).astype(BF16).astype(F32)
        ctx_ref[r] = (acc_s[r] * (keep / total) + prob * value_new).astype(BF16)
    h1 = activate(1, g1)
    h2 = activate(2, g2)
    wdcp.wait()
    for cp in h0 + h1 + h2:
        cp.wait_recv()

    def down(t, _):
        col = pl.ds(pl.multiple_of(t * 256, 256), 256)
        part = jnp.dot(hs[...].reshape(rows, -1), wd[:, col], preferred_element_type=F32)
        dp[:, :, :, :, col] = part.astype(BF16).reshape(NC, NZ, NY, SLAB, 256)
        return 0

    lax.fori_loop(0, d_dev // 256, down, 0)
    core = rcopy(dp.at[oc], dr, dev(dc=1))
    core.wait_recv()
    reduce_core(dp, dr, ds_, d_dev)
    r1 = reduce_first(ds_, azr, byr, ca, cb)
    for cp in r1:
        cp.wait_recv()
    r2 = reduce_second(ds_, azr, byr, ta, tb, tar, tbr, ca, cb)
    for cp in r2:
        cp.wait_recv()
    low, high = reduce_last(ta, tb, tar, tbr)
    for j in range(NX):
        fx[j, :, ca] = low[4 * j : 4 * j + 4]
        fx[j, :, cb] = high[4 * j : 4 * j + 4]
    r3 = [rcopy(fx.at[lax.rem(x + i, NX)], fxr.at[x], dev(dx=i)) for i in range(1, NX)]
    fxr[x] = fx[x]
    for cp in r3:
        cp.wait_recv()
    for j in range(NX):
        cols = pl.ds(j * d_dev, d_dev)
        mixed_ref[:, cols] = (tokens_ref[:, cols].astype(F32) + fxr[j]).astype(BF16)
    for cp in sent:
        cp.wait_send()


def body(tokens, gain, w_gate, w_up, w_down, w_kv, queries, key_cache, value_cache, lengths):
    batch, width = tokens.shape
    d_dev, hid = w_gate.shape
    span = key_cache.shape[1]
    n_tiles = hid // TILE
    rows = NC * NZ * NY * SLAB
    chunk = rows // NX
    half = d_dev // 2
    per = n_tiles // GRAN
    vm = pl.BlockSpec(memory_space=pltpu.VMEM)
    hbm = pl.BlockSpec(memory_space=pltpu.HBM)
    mixed, context = pl.pallas_call(
        step_kernel,
        name="step",
        out_shape=(
            jax.ShapeDtypeStruct((batch, width), BF16),
            jax.ShapeDtypeStruct((batch, HEADS, HD), BF16),
        ),
        in_specs=[vm, vm, vm, pl.BlockSpec(memory_space=pltpu.SMEM), vm] + [hbm] * 5,
        out_specs=(vm, vm),
        scratch_shapes=[
            pltpu.VMEM((batch, span, HD), BF16),
            pltpu.VMEM((batch, span, HD), BF16),
            pltpu.VMEM((n_tiles, d_dev, 2 * TILE), BF16),
            pltpu.VMEM((hid, d_dev), BF16),
            pltpu.VMEM((NX, 4, d_dev), F32),
            pltpu.VMEM((NX, 4, d_dev), F32),
            pltpu.VMEM((NC, NZ, NY, SLAB, d_dev), BF16),
            pltpu.VMEM((2 * TILE, 2 * HD), BF16),
            pltpu.VMEM((NC, NZ, NY, SLAB, 2 * HD), F32),
            pltpu.VMEM((NZ, NY, SLAB, 2 * HD), F32),
            pltpu.VMEM((NZ, NY, SLAB, 2 * HD), F32),
            pltpu.VMEM((NZ - 1, NY, SLAB, HD), F32),
            pltpu.VMEM((NY - 1, NZ, SLAB, HD), F32),
            pltpu.VMEM((2, NY, SLAB, HD), F32),
            pltpu.VMEM((2, NY - 1, SLAB, HD), F32),
            pltpu.VMEM((NX, 4, 2 * HD), F32),
            pltpu.VMEM((NX - 1, 4, 2 * HD), F32),
            pltpu.VMEM((NX, GRAN, chunk, per * 2 * TILE), BF16),
            pltpu.VMEM((NX - 1, GRAN, chunk, per * 2 * TILE), BF16),
            pltpu.VMEM((NX, chunk, hid), BF16),
            pltpu.VMEM((NC, NZ, NY, SLAB, d_dev), BF16),
            pltpu.VMEM((NZ, NY, SLAB, d_dev), BF16),
            pltpu.VMEM((NZ, NY, SLAB, d_dev), BF16),
            pltpu.VMEM((NZ - 1, NY, SLAB, half), BF16),
            pltpu.VMEM((NY - 1, NZ, SLAB, half), BF16),
            pltpu.VMEM((NY, SLAB, half), BF16),
            pltpu.VMEM((NZ, SLAB, half), BF16),
            pltpu.VMEM((NY - 1, SLAB, half), BF16),
            pltpu.VMEM((NZ - 1, SLAB, half), BF16),
            pltpu.VMEM((NX, 4, d_dev), F32),
            pltpu.VMEM((NX, 4, d_dev), F32),
            pltpu.VMEM((batch, HEADS, 128), F32),
            pltpu.VMEM((batch, HEADS, 128), F32),
            pltpu.VMEM((batch, HEADS, HD), F32),
            pltpu.SemaphoreType.DMA((96,)),
            pltpu.SemaphoreType.DMA((96,)),
            pltpu.SemaphoreType.DMA((5, n_tiles)),
        ],
        compiler_params=pltpu.CompilerParams(
            collective_id=0, has_side_effects=True, vmem_limit_bytes=60 << 20
        ),
    )(
        tokens, gain.reshape(1, -1), queries.reshape(batch, HEADS, HD), lengths, w_kv[0],
        w_gate, w_up, w_down, key_cache, value_cache,
    )
    return mixed, context.reshape(batch, HEADS * HD)


def solution(mesh):
    return jax.shard_map(
        body,
        mesh=mesh,
        in_specs=(
            P(("gx", "gy"), None),
            P(),
            P("gy", "gx"),
            P("gy", "gx"),
            P("gx", "gy"),
            P("gy", "gx", None),
            P(("gx", "gy"), None),
            P(("gx", "gy"), None, None),
            P(("gx", "gy"), None, None),
            P(("gx", "gy")),
        ),
        out_specs=(P(("gx", "gy"), None), P(("gx", "gy"), None)),
        check_vma=False,
    )
```

```python
import functools
import math

import jax
import jax.numpy as jnp
from jax import lax
from jax.experimental import pallas as pl
from jax.experimental.pallas import tpu as pltpu
from jax.sharding import PartitionSpec as P

MESH = pl.DeviceIdType.MESH
HD = 256
HEADS = 48
NZ, NY, NC, NX = 4, 4, 2, 4
SLAB = 16
TILE = 128
GRAN = 3
GRP = 3
F32 = jnp.float32
BF16 = jnp.bfloat16


def step_kernel(
    tokens_ref, gain_ref, q_ref, len_ref, wkv_ref,
    wg_hbm, wu_hbm, wd_hbm, k_hbm, v_hbm,
    ffn_ref, ctx_ref,
    kbuf, vbuf, wgu, wd, nx, xr, xa, wpad, kp, kr, ks, kzr, kyr, kts, kt2r, kx, kxr,
    ps, rf, rn, hs, own, dp, dr, ds_, azr, byr, ta, tb, tar, tbr, fx, fxr,
    q_s, c_s, m_s, l_s, acc_s, ssem, rsem, lsem,
):
    d_dev = xa.shape[-1]
    half = d_dev // 2
    gx = lax.axis_index("gx")
    x = lax.axis_index("gy")
    z = gx // (NY * NC)
    y = lax.rem(gx // NC, NY)
    c = lax.rem(gx, NC)
    oc = 1 - c

    def dev(dz=0, dy=0, dc=0, dx=0):
        zz, yy, cc = lax.rem(z + dz, NZ), lax.rem(y + dy, NY), lax.rem(c + dc, NC)
        return ((zz * NY + yy) * NC + cc, lax.rem(x + dx, NX))

    counter = [0]
    sent = []

    def rcopy(src, dst, device):
        i = counter[0]
        counter[0] += 1
        cp = pltpu.make_async_remote_copy(
            src_ref=src, dst_ref=dst, send_sem=ssem.at[i], recv_sem=rsem.at[i],
            device_id=device, device_id_type=MESH,
        )
        cp.start()
        sent.append(cp)
        return cp

    def arrive(cps):
        for cp in cps:
            cp.wait_recv()

    bar = pltpu.get_barrier_semaphore()
    peers = (
        [dev(dz=i) for i in range(1, NZ)] + [dev(dy=i) for i in range(1, NY)]
        + [dev(dx=i) for i in range(1, NX)] + [dev(dc=1)]
    )
    for peer in peers:
        pl.semaphore_signal(bar, inc=1, device_id=peer, device_id_type=MESH)

    values = tokens_ref[...].astype(F32)
    centred = values - jnp.mean(values, axis=-1, keepdims=True)
    spread = jnp.mean(centred * centred, axis=-1, keepdims=True)
    normed = centred * lax.rsqrt(spread + 1e-05) * gain_ref[...]
    for j in range(NX):
        nx[j] = normed[:, j * d_dev : (j + 1) * d_dev]

    pl.semaphore_wait(bar, len(peers))

    cps = [
        rcopy(nx.at[lax.rem(x + i, NX)], xr.at[x], dev(dx=i)) for i in range(1, NX)
    ]
    xr[x] = nx[x]

    kcp = [pltpu.make_async_copy(k_hbm.at[r], kbuf.at[r], lsem.at[0, r]) for r in range(4)]
    vcp = [pltpu.make_async_copy(v_hbm.at[r], vbuf.at[r], lsem.at[1, r]) for r in range(4)]
    for r in range(4):
        kcp[r].start()
        vcp[r].start()
    n_tiles = wgu.shape[0]

    def weight_copies(t):
        cols = pl.ds(pl.multiple_of(t * TILE, TILE), TILE)
        return (
            pltpu.make_async_copy(wg_hbm.at[:, cols], wgu.at[t, :, pl.ds(0, TILE)], lsem.at[2, t]),
            pltpu.make_async_copy(wu_hbm.at[:, cols], wgu.at[t, :, pl.ds(TILE, TILE)], lsem.at[3, t]),
        )

    for t in range(n_tiles):
        for cp in weight_copies(t):
            cp.start()
    wdcp = pltpu.make_async_copy(wd_hbm, wd, lsem.at[4, 0])
    wdcp.start()

    arrive(cps)
    xa[c, z, y] = jnp.concatenate([xr[j] for j in range(NX)], axis=0).astype(BF16)

    ca, cb = pl.ds(0, half), pl.ds(half, half)
    st1 = [
        rcopy(xa.at[c, z, y, :, ca], xa.at[c, z, y, :, ca], dev(dy=i)) for i in range(1, NY)
    ] + [
        rcopy(xa.at[c, z, y, :, cb], xa.at[c, z, y, :, cb], dev(dz=i)) for i in range(1, NZ)
    ]

    scale = 1.0 / math.sqrt(HD)

    def spread_heads(h, _):
        row = q_ref[:, pl.ds(pl.multiple_of(h * HD, HD), HD)].astype(F32)
        for r in range(4):
            q_s[r, pl.ds(h, 1), :] = row[r : r + 1]
        return 0

    lax.fori_loop(0, HEADS, spread_heads, 0)

    def attend(r):
        s = lax.dot_general(
            q_s[r].astype(BF16), kbuf[r], (((1,), (1,)), ((), ())), preferred_element_type=F32
        ) * scale
        live = lax.broadcasted_iota(jnp.int32, s.shape, 1) < len_ref[r]
        s = jnp.where(live, s, -jnp.inf)
        m = jnp.max(s, axis=-1, keepdims=True)
        p = jnp.exp(s - m)
        l = jnp.sum(p, axis=-1, keepdims=True)
        m_s[r] = jnp.broadcast_to(m, m_s.shape[1:])
        l_s[r] = jnp.broadcast_to(l, l_s.shape[1:])
        acc_s[r] = jnp.dot(p.astype(BF16), vbuf[r], preferred_element_type=F32)

    arrive(st1)
    st2 = [
        rcopy(xa.at[c, z, :, :, ca], xa.at[c, z, :, :, ca], dev(dz=i)) for i in range(1, NZ)
    ] + [
        rcopy(xa.at[c, :, y, :, cb], xa.at[c, :, y, :, cb], dev(dy=i)) for i in range(1, NY)
    ]
    for r in range(4):
        kcp[r].wait()
        vcp[r].wait()
    lax.fori_loop(0, 4, lambda r, _: (attend(r), 0)[1], 0)

    span = wkv_ref.shape[0]
    offset = gx * span
    start = jnp.minimum(offset // TILE, d_dev // TILE - 2) * TILE
    wide = jnp.concatenate(
        [wkv_ref[...].astype(F32), jnp.zeros((2 * TILE - span, 2 * HD), F32)], axis=0
    )
    wpad[...] = pltpu.roll(wide, offset - start, axis=0).astype(BF16)

    arrive(st2)
    sib = rcopy(xa.at[c], xa.at[c], dev(dc=1))

    blk = NZ * NY * SLAB
    rows = NC * blk

    def reduce_core(mine, other, out):
        def add(i, _):
            a, b = i // NY, lax.rem(i, NY)
            out[a, b] = (mine[a, b].astype(F32) + other[a, b].astype(F32)).astype(out.dtype)
            return 0

        lax.fori_loop(0, NZ * NY, add, 0)

    def reduce_first(out, az, by, ha, hb):
        return [
            rcopy(out.at[lax.rem(z + i, NZ), :, :, ha], az.at[i - 1], dev(dz=i)) for i in range(1, NZ)
        ] + [
            rcopy(out.at[:, lax.rem(y + i, NY), :, hb], by.at[i - 1], dev(dy=i)) for i in range(1, NY)
        ]

    def reduce_second(out, az, by, ta, tb, tar, tbr, ha, hb):
        def add_a(b, _):
            total = out[z, b, :, ha].astype(F32)
            for i in range(NZ - 1):
                total += az[i, b].astype(F32)
            ta[b] = total.astype(ta.dtype)
            return 0

        def add_b(a, _):
            total = out[a, y, :, hb].astype(F32)
            for i in range(NY - 1):
                total += by[i, a].astype(F32)
            tb[a] = total.astype(tb.dtype)
            return 0

        lax.fori_loop(0, NY, add_a, 0)
        cps = [rcopy(ta.at[lax.rem(y + i, NY)], tar.at[i - 1], dev(dy=i)) for i in range(1, NY)]
        lax.fori_loop(0, NZ, add_b, 0)
        return cps + [rcopy(tb.at[lax.rem(z + i, NZ)], tbr.at[i - 1], dev(dz=i)) for i in range(1, NZ)]

    def reduce_last(ta, tb, tar, tbr):
        a, b = ta[y].astype(F32), tb[z].astype(F32)
        for i in range(NY - 1):
            a += tar[i].astype(F32)
        for i in range(NZ - 1):
            b += tbr[i].astype(F32)
        return a, b

    per = n_tiles // GRAN
    chunk = blk // NX
    part_rows = chunk // 2
    upper, lower = pl.ds(0, part_rows), pl.ds(part_rows, part_rows)
    right, left = dev(dx=1), dev(dx=NX - 1)
    xp, xm, xf = lax.rem(x + 1, NX), lax.rem(x + NX - 1, NX), lax.rem(x + 2, NX)

    def gate_up(u):
        b, g = divmod(u, GRAN)
        block = c if b == 0 else oc

        def tile(t, _):
            col = pl.ds(pl.multiple_of(t * 2 * TILE, 2 * TILE), 2 * TILE)
            if b == 0:
                for cp in weight_copies(g * per + t):
                    cp.wait()
            part = jnp.dot(
                xa[block].reshape(blk, d_dev), wgu[g * per + t], preferred_element_type=F32
            )
            for k in range(NX):
                ps[u, k, :, col] = part[k * chunk : (k + 1) * chunk].astype(BF16)
            return 0

        lax.fori_loop(0, per, tile, 0)
        far = [
            rcopy(ps.at[u, xf, upper], rf.at[u, 0], right),
            rcopy(ps.at[u, xf, lower], rf.at[u, 1], left),
        ]
        near = [
            rcopy(ps.at[u, xp, lower], rn.at[u, 0, lower], right),
            rcopy(ps.at[u, xm, upper], rn.at[u, 1, upper], left),
        ]
        return far, near

    def pass_on(u, far):
        out = []
        for i, (k, part, device) in enumerate(((xp, upper, right), (xm, lower, left))):
            far[i].wait_recv()
            ps[u, k, part] = (ps[u, k, part].astype(F32) + rf[u, i].astype(F32)).astype(BF16)
            out.append(rcopy(ps.at[u, k, part], rn.at[u, i, part], device))
        return out

    def activate(u, cps):
        b, g = divmod(u, GRAN)
        arrive(cps)
        for t in range(per):
            col = pl.ds(t * 2 * TILE, 2 * TILE)
            total = ps[u, x, :, col].astype(F32)
            for i in range(2):
                total += rn[u, i, :, col].astype(F32)
            gate, up = total[:, :TILE], total[:, TILE:]
            hs[b, x, :, pl.ds((g * per + t) * TILE, TILE)] = (
                gate / (1.0 + jnp.exp(-gate)) * up
            ).astype(BF16)
        cols = pl.ds(g * per * TILE, per * TILE)
        return [
            rcopy(hs.at[b, x, :, cols], hs.at[b, x, :, cols], right),
            rcopy(hs.at[b, x, :, cols], hs.at[b, x, :, cols], left),
        ]

    def forward(u, cps):
        b, g = divmod(u, GRAN)
        cols = pl.ds(g * per * TILE, per * TILE)
        out = []
        for cp, k, part, device in zip(cps, (xm, xp), (upper, lower), (right, left)):
            cp.wait_recv()
            out.append(rcopy(hs.at[b, k, part, cols], hs.at[b, k, part, cols], device))
        return out

    grp_cols = d_dev // GRP

    def down(b, grp):
        into = own if b == 0 else dp

        def tile(t, _):
            src = pl.ds(pl.multiple_of(grp * grp_cols + t * 256, 256), 256)
            dst = pl.ds(pl.multiple_of(t * 256, 256), 256)
            part = jnp.dot(hs[b].reshape(blk, -1), wd[:, src], preferred_element_type=F32)
            into[grp, :, :, :, dst] = part.astype(into.dtype).reshape(NZ, NY, SLAB, 256)
            return 0

        lax.fori_loop(0, grp_cols // 256, tile, 0)

    units = NC * GRAN
    far, near, passed, sent_h, fwd = {}, {}, {}, {}, {}

    def s0(u):
        far[u], near[u] = gate_up(u)

    def s1(u):
        passed[u] = pass_on(u, far[u])

    def s2(u):
        sent_h[u] = activate(u, near[u] + passed[u])

    def s3(u):
        fwd[u] = forward(u, sent_h[u])

    s0(0)
    s0(1)
    s1(0)
    s0(2)
    s1(1)
    sib.wait_recv()

    ka, kb = pl.ds(0, HD), pl.ds(HD, HD)
    xwin = xa[:, :, :, :, pl.ds(pl.multiple_of(start, TILE), 2 * TILE)].reshape(rows, 2 * TILE)
    kp[...] = jnp.dot(xwin, wpad[...], preferred_element_type=F32).reshape(kp.shape)
    kv_core = rcopy(kp.at[oc], kr, dev(dc=1))

    s0(3)
    s1(2)
    kv_core.wait_recv()
    reduce_core(kp.at[c], kr, ks)
    kv1 = reduce_first(ks, kzr, kyr, ka, kb)
    s2(0)
    s0(4)
    s1(3)
    s2(1)
    s3(0)
    arrive(kv1)
    kv2 = reduce_second(
        ks, kzr, kyr, kts.at[0], kts.at[1], kt2r.at[0], kt2r.at[1], ka, kb
    )
    s0(5)
    s1(4)
    s2(2)
    s3(1)
    arrive(kv2)
    key_sum, value_sum = reduce_last(kts.at[0], kts.at[1], kt2r.at[0], kt2r.at[1])
    for j in range(NX):
        kx[j] = jnp.concatenate([key_sum[4 * j : 4 * j + 4], value_sum[4 * j : 4 * j + 4]], axis=1)
    kv3 = [rcopy(kx.at[lax.rem(x + i, NX)], kxr.at[i - 1], dev(dx=i)) for i in range(1, NX)]
    s1(5)
    s2(3)
    s3(2)
    arrive(kv3)
    fresh = kx[x]
    for i in range(NX - 1):
        fresh += kxr[i]
    fresh = fresh.astype(BF16).astype(F32)
    for r in range(4):
        key_new, value_new = fresh[r : r + 1, :HD], fresh[r : r + 1, HD:]
        s_new = jnp.sum(q_s[r] * key_new, axis=-1, keepdims=True) * scale
        m_old = m_s[r][:, :1]
        m = jnp.maximum(m_old, s_new)
        keep, mine = jnp.exp(m_old - m), jnp.exp(s_new - m)
        total = l_s[r][:, :1] * keep + mine
        prob = (mine / total).astype(BF16).astype(F32)
        c_s[r] = acc_s[r] * (keep / total) + prob * value_new

    s2(4)
    s3(3)

    def gather_heads(h, _):
        row = jnp.concatenate([c_s[r, pl.ds(h, 1), :] for r in range(4)], axis=0)
        ctx_ref[:, pl.ds(pl.multiple_of(h * HD, HD), HD)] = row
        return 0

    lax.fori_loop(0, HEADS, gather_heads, 0)
    wdcp.wait()
    arrive(fwd[0] + fwd[1] + fwd[2])
    down(0, 0)
    s2(5)
    s3(4)
    down(0, 1)
    s3(5)
    down(0, 2)
    arrive(fwd[3] + fwd[4] + fwd[5])

    ga, gb = pl.ds(0, grp_cols // 2), pl.ds(grp_cols // 2, grp_cols // 2)
    core, r1, r2 = [], [], []

    def first(i):
        core[i].wait_recv()
        reduce_core(own.at[i], dr.at[i], ds_.at[i])
        r1.append(reduce_first(ds_.at[i], azr.at[i], byr.at[i], ga, gb))

    for i in range(GRP):
        down(1, i)
        core.append(rcopy(dp.at[i], dr.at[i], dev(dc=1)))
        if i:
            first(i - 1)
    first(GRP - 1)
    for i in range(GRP):
        arrive(r1[i])
        r2.append(reduce_second(
            ds_.at[i], azr.at[i], byr.at[i], ta.at[i], tb.at[i], tar.at[i], tbr.at[i], ga, gb
        ))
    for i in range(GRP):
        arrive(r2[i])
        low, high = reduce_last(ta.at[i], tb.at[i], tar.at[i], tbr.at[i])
        for j in range(NX):
            fx[j, :, pl.ds(i * grp_cols, grp_cols // 2)] = low[4 * j : 4 * j + 4]
            fx[j, :, pl.ds(i * grp_cols + grp_cols // 2, grp_cols // 2)] = high[4 * j : 4 * j + 4]
    r3 = [rcopy(fx.at[lax.rem(x + i, NX)], fxr.at[x], dev(dx=i)) for i in range(1, NX)]
    fxr[x] = fx[x]
    arrive(r3)
    for j in range(NX):
        ffn_ref[:, pl.ds(j * d_dev, d_dev)] = fxr[j]
    for cp in sent:
        cp.wait_send()


def body(tokens, gain, w_gate, w_up, w_down, w_kv, queries, key_cache, value_cache, lengths):
    batch, width = tokens.shape
    d_dev, hid = w_gate.shape
    span = key_cache.shape[1]
    n_tiles = hid // TILE
    blk = NZ * NY * SLAB
    chunk = blk // NX
    per = n_tiles // GRAN
    units = NC * GRAN
    gc = d_dev // GRP
    vm = pl.BlockSpec(memory_space=pltpu.VMEM)
    hbm = pl.BlockSpec(memory_space=pltpu.HBM)
    ffn, context = pl.pallas_call(
        step_kernel,
        name="step",
        out_shape=(
            jax.ShapeDtypeStruct((batch, width), F32),
            jax.ShapeDtypeStruct((batch, HEADS * HD), F32),
        ),
        in_specs=[vm, vm, vm, pl.BlockSpec(memory_space=pltpu.SMEM), vm] + [hbm] * 5,
        out_specs=(vm, vm),
        scratch_shapes=[
            pltpu.VMEM((batch, span, HD), BF16),
            pltpu.VMEM((batch, span, HD), BF16),
            pltpu.VMEM((n_tiles, d_dev, 2 * TILE), BF16),
            pltpu.VMEM((hid, d_dev), BF16),
            pltpu.VMEM((NX, 4, d_dev), F32),
            pltpu.VMEM((NX, 4, d_dev), F32),
            pltpu.VMEM((NC, NZ, NY, SLAB, d_dev), BF16),
            pltpu.VMEM((2 * TILE, 2 * HD), BF16),
            pltpu.VMEM((NC, NZ, NY, SLAB, 2 * HD), F32),
            pltpu.VMEM((NZ, NY, SLAB, 2 * HD), F32),
            pltpu.VMEM((NZ, NY, SLAB, 2 * HD), F32),
            pltpu.VMEM((NZ - 1, NY, SLAB, HD), F32),
            pltpu.VMEM((NY - 1, NZ, SLAB, HD), F32),
            pltpu.VMEM((2, NY, SLAB, HD), F32),
            pltpu.VMEM((2, NY - 1, SLAB, HD), F32),
            pltpu.VMEM((NX, 4, 2 * HD), F32),
            pltpu.VMEM((NX - 1, 4, 2 * HD), F32),
            pltpu.VMEM((units, NX, chunk, per * 2 * TILE), BF16),
            pltpu.VMEM((units, 2, chunk // 2, per * 2 * TILE), BF16),
            pltpu.VMEM((units, 2, chunk, per * 2 * TILE), BF16),
            pltpu.VMEM((NC, NX, chunk, hid), BF16),
            pltpu.VMEM((GRP, NZ, NY, SLAB, gc), F32),
            pltpu.VMEM((GRP, NZ, NY, SLAB, gc), BF16),
            pltpu.VMEM((GRP, NZ, NY, SLAB, gc), BF16),
            pltpu.VMEM((GRP, NZ, NY, SLAB, gc), BF16),
            pltpu.VMEM((GRP, NZ - 1, NY, SLAB, gc // 2), BF16),
            pltpu.VMEM((GRP, NY - 1, NZ, SLAB, gc // 2), BF16),
            pltpu.VMEM((GRP, NY, SLAB, gc // 2), BF16),
            pltpu.VMEM((GRP, NZ, SLAB, gc // 2), BF16),
            pltpu.VMEM((GRP, NY - 1, SLAB, gc // 2), BF16),
            pltpu.VMEM((GRP, NZ - 1, SLAB, gc // 2), BF16),
            pltpu.VMEM((NX, 4, d_dev), F32),
            pltpu.VMEM((NX, 4, d_dev), F32),
            pltpu.VMEM((batch, HEADS, HD), F32),
            pltpu.VMEM((batch, HEADS, HD), F32),
            pltpu.VMEM((batch, HEADS, 128), F32),
            pltpu.VMEM((batch, HEADS, 128), F32),
            pltpu.VMEM((batch, HEADS, HD), F32),
            pltpu.SemaphoreType.DMA((144,)),
            pltpu.SemaphoreType.DMA((144,)),
            pltpu.SemaphoreType.DMA((5, n_tiles)),
        ],
        compiler_params=pltpu.CompilerParams(
            collective_id=0, has_side_effects=True, vmem_limit_bytes=60 << 20
        ),
    )(
        tokens, gain.reshape(1, -1), queries, lengths, w_kv[0],
        w_gate, w_up, w_down, key_cache, value_cache,
    )
    mixed = (tokens.astype(F32) + ffn).astype(BF16)
    return mixed, context.astype(BF16)


def solution(mesh):
    return jax.shard_map(
        body,
        mesh=mesh,
        in_specs=(
            P(("gx", "gy"), None),
            P(),
            P("gy", "gx"),
            P("gy", "gx"),
            P("gx", "gy"),
            P("gy", "gx", None),
            P(("gx", "gy"), None),
            P(("gx", "gy"), None, None),
            P(("gx", "gy"), None, None),
            P(("gx", "gy")),
        ),
        out_specs=(P(("gx", "gy"), None), P(("gx", "gy"), None)),
        check_vma=False,
    )
```

```python
import functools
import math

import jax
import jax.numpy as jnp
from jax import lax
from jax.experimental import pallas as pl
from jax.experimental.pallas import tpu as pltpu
from jax.sharding import PartitionSpec as P

MESH = pl.DeviceIdType.MESH
HD = 256
HEADS = 48
NZ, NY, NC, NX = 4, 4, 2, 4
SLAB = 16
TILE = 128
GRAN = 3
F32 = jnp.float32
BF16 = jnp.bfloat16


def step_kernel(
    len_ref, tok_hbm, gain_hbm, q_hbm, wkv_hbm, wg_hbm, wu_hbm, wd_hbm, k_hbm, v_hbm,
    ffn_ref, ctx_ref,
    tokens_ref, gain_ref, q_ref, wkv_ref,
    kbuf, vbuf, wgu, wd, nx, xr, xa, wpad, kp, kr, ks, kz, kt, ktr, kx, kxr,
    ps, rf, rn, hs, own, dp, dr, ds_, az, tt, tr, fx, fr,
    q_s, c_s, m_s, l_s, acc_s, ssem, rsem, lsem,
):
    d_dev = xa.shape[-1]
    half = d_dev // 2
    gx = lax.axis_index("gx")
    x = lax.axis_index("gy")
    z = gx // (NY * NC)
    y = lax.rem(gx // NC, NY)
    c = lax.rem(gx, NC)
    oc = 1 - c

    def at(zz, yy, cc, xx):
        return ((zz * NY + yy) * NC + cc, xx)

    def dev(dz=0, dy=0, dx=0):
        return at(lax.rem(z + dz, NZ), lax.rem(y + dy, NY), c, lax.rem(x + dx, NX))

    sibling = at(z, y, oc, x)
    gather_first = [dev(dy=i * oc, dz=i * c) for i in range(1, NZ)]
    gather_second = [dev(dz=i * oc, dy=i * c) for i in range(1, NZ)]
    fi, si = z * oc + y * c, y * oc + z * c

    send_count, recv_count, finals = [0], [0], []

    def recvs(n):
        recv_count[0] += n
        return recv_count[0] - n

    def describe(src, dst, device, si_, ri):
        return pltpu.make_async_remote_copy(
            src_ref=src, dst_ref=dst, send_sem=ssem.at[si_], recv_sem=rsem.at[ri],
            device_id=device, device_id_type=MESH,
        )

    def rcopy(src, dst, device, ri=None):
        i = send_count[0]
        send_count[0] += 1
        cp = describe(src, dst, device, i, recvs(1) if ri is None else ri)
        cp.start()
        finals.append(cp.wait_send)
        return cp

    def arrive(cps):
        for cp in cps:
            cp.wait_recv()

    bar = pltpu.get_barrier_semaphore()
    peers = (
        [dev(dz=i) for i in range(1, NZ)] + [dev(dy=i) for i in range(1, NY)]
        + [at(z, y, h, lax.rem(x + i, NX)) for i in range(1, NX) for h in range(NC)] + [sibling]
    )
    for peer in peers:
        pl.semaphore_signal(bar, inc=1, device_id=peer, device_id_type=MESH)

    small = [
        pltpu.make_async_copy(src, dst, lsem.at[4, 1 + i]) for i, (src, dst) in enumerate(
            ((tok_hbm, tokens_ref), (gain_hbm, gain_ref), (q_hbm, q_ref), (wkv_hbm, wkv_ref))
        )
    ]
    kcp = [pltpu.make_async_copy(k_hbm.at[r], kbuf.at[r], lsem.at[0, r]) for r in range(4)]
    vcp = [pltpu.make_async_copy(v_hbm.at[r], vbuf.at[r], lsem.at[1, r]) for r in range(4)]
    per = wgu.shape[2] // (2 * TILE)
    n_tiles = per * GRAN

    def weight_copies(t):
        cols = pl.ds(t * TILE, TILE)
        g, lo = t // per, t % per * 2 * TILE
        return (
            pltpu.make_async_copy(wg_hbm.at[:, cols], wgu.at[g, :, pl.ds(lo, TILE)], lsem.at[2, t]),
            pltpu.make_async_copy(
                wu_hbm.at[:, cols], wgu.at[g, :, pl.ds(lo + TILE, TILE)], lsem.at[3, t]
            ),
        )

    for cp in small:
        cp.start()
    for r in range(4):
        kcp[r].start()
        vcp[r].start()
    for t in range(n_tiles):
        for cp in weight_copies(t):
            cp.start()
    wdcp = pltpu.make_async_copy(wd_hbm, wd, lsem.at[4, 0])
    wdcp.start()

    small[0].wait()
    small[1].wait()
    values = tokens_ref[...].astype(F32)
    centred = values - jnp.mean(values, axis=-1, keepdims=True)
    spread_of = jnp.mean(centred * centred, axis=-1, keepdims=True)
    normed = centred * lax.rsqrt(spread_of + 1e-05) * gain_ref[...]
    for j in range(NX):
        for h in range(NC):
            lo = j * d_dev + h * half
            nx[h, j] = normed[:, lo : lo + half]

    pl.semaphore_wait(bar, len(peers))

    def spread(src, dst):
        base = recvs(7)
        for h in range(NC):
            for i in range(1, NX):
                to = lax.rem(x + i, NX)
                rcopy(src.at[h, to], dst.at[c, x], at(z, y, h, to), base + c * 3 + i - 1)
        rcopy(src.at[oc, x], dst.at[c, x], sibling, base + 6)
        dst[c, x] = src[c, x]
        out = [
            describe(src.at[0, 0], dst.at[h, lax.rem(x + NX - i, NX)], sibling, 0, base + h * 3 + i - 1)
            for h in range(NC) for i in range(1, NX)
        ]
        return out + [describe(src.at[0, 0], dst.at[oc, x], sibling, 0, base + 6)]

    cps = spread(nx, xr)
    c0, c1 = pl.ds(0, half), pl.ds(half, half)
    ch = pl.ds(pl.multiple_of(c * half, TILE), half)
    och = pl.ds(pl.multiple_of(oc * half, TILE), half)
    arrive(cps)

    def gather1(b):
        xa[b, z, y, :, ch] = jnp.concatenate([xr[b, j] for j in range(NX)], axis=0).astype(BF16)
        return [
            rcopy(xa.at[b, z, y, :, ch], xa.at[b, z, y, :, ch], gather_first[i]) for i in range(NZ - 1)
        ]

    def gather2(b):
        sbase, rbase = send_count[0], recvs(NZ - 1)
        send_count[0] += NZ - 1

        def each(do):
            for core, ref in ((0, xa.at[b, z, :, :, c0]), (1, xa.at[b, :, y, :, c1])):
                @pl.when(c == core)
                def _():
                    for i in range(NZ - 1):
                        do(describe(ref, ref, gather_second[i], sbase + i, rbase + i))

        each(lambda cp: cp.start())
        finals.append(lambda: each(lambda cp: cp.wait_send()))
        return lambda: each(lambda cp: cp.wait_recv())

    def gather3(b):
        return rcopy(xa.at[b, :, :, :, ch], xa.at[b, :, :, :, ch], sibling)

    g1 = [gather1(b) for b in range(NC)]
    scale = 1.0 / math.sqrt(HD)

    def spread_heads(h, _):
        row = q_ref[:, pl.ds(pl.multiple_of(h * HD, HD), HD)].astype(F32)
        for r in range(4):
            q_s[r, pl.ds(h, 1), :] = row[r : r + 1]
        return 0

    def attend(r):
        kcp[r].wait()
        vcp[r].wait()
        s = lax.dot_general(
            q_s[r].astype(BF16), kbuf[r], (((1,), (1,)), ((), ())), preferred_element_type=F32
        ) * scale
        live = lax.broadcasted_iota(jnp.int32, s.shape, 1) < len_ref[r]
        s = jnp.where(live, s, -jnp.inf)
        m = jnp.max(s, axis=-1, keepdims=True)
        p = jnp.exp(s - m)
        l = jnp.sum(p, axis=-1, keepdims=True)
        m_s[r] = jnp.broadcast_to(m, m_s.shape[1:])
        l_s[r] = jnp.broadcast_to(l, l_s.shape[1:])
        acc_s[r] = jnp.dot(p.astype(BF16), vbuf[r], preferred_element_type=F32)

    small[2].wait()
    lax.fori_loop(0, HEADS, spread_heads, 0)
    attend(0)
    attend(1)
    arrive(g1[0])
    g2 = [gather2(0)]
    arrive(g1[1])
    g2.append(gather2(1))
    attend(2)
    attend(3)

    small[3].wait()
    span = wkv_ref.shape[0]
    offset = gx * span
    start = jnp.minimum(offset // TILE, d_dev // TILE - 2) * TILE
    wide = jnp.concatenate(
        [wkv_ref[...].astype(F32), jnp.zeros((2 * TILE - span, 2 * HD), F32)], axis=0
    )
    wpad[...] = pltpu.roll(wide, offset - start, axis=0).astype(BF16)

    g2[0]()
    sib0 = gather3(0)
    sib0.wait_recv()

    blk = NZ * NY * SLAB

    chunk = blk // NX
    part_rows = chunk // 2
    upper, lower = pl.ds(0, part_rows), pl.ds(part_rows, part_rows)
    right, left = dev(dx=1), dev(dx=NX - 1)
    xp, xm, xf = lax.rem(x + 1, NX), lax.rem(x + NX - 1, NX), lax.rem(x + 2, NX)

    def gate_up(u):
        b, g = divmod(u, GRAN)

        if b == 0:
            for t in range(per):
                for cp in weight_copies(g * per + t):
                    cp.wait()
        part = jnp.dot(xa[b].reshape(blk, d_dev), wgu[g], preferred_element_type=F32)
        for k in range(NX):
            ps[u, k] = part[k * chunk : (k + 1) * chunk].astype(BF16)
        far = [
            rcopy(ps.at[u, xf, upper], rf.at[u, 0], right),
            rcopy(ps.at[u, xf, lower], rf.at[u, 1], left),
        ]
        near = [
            rcopy(ps.at[u, xp, lower], rn.at[u, 0, lower], right),
            rcopy(ps.at[u, xm, upper], rn.at[u, 1, upper], left),
        ]
        return far, near

    def pass_on(u, far):
        out = []
        for i, (k, part, device) in enumerate(((xp, upper, right), (xm, lower, left))):
            far[i].wait_recv()
            ps[u, k, part] = (ps[u, k, part].astype(F32) + rf[u, i].astype(F32)).astype(BF16)
            out.append(rcopy(ps.at[u, k, part], rn.at[u, i, part], device))
        return out

    def activate(u, cps):
        b, g = divmod(u, GRAN)
        arrive(cps)
        for t in range(per):
            col = pl.ds(t * 2 * TILE, 2 * TILE)
            total = ps[u, x, :, col].astype(F32)
            for i in range(2):
                total += rn[u, i, :, col].astype(F32)
            gate, up = total[:, :TILE], total[:, TILE:]
            hs[b, x, :, pl.ds((g * per + t) * TILE, TILE)] = (
                gate / (1.0 + jnp.exp(-gate)) * up
            ).astype(BF16)
        cols = pl.ds(g * per * TILE, per * TILE)
        return [
            rcopy(hs.at[b, x, :, cols], hs.at[b, x, :, cols], right),
            rcopy(hs.at[b, x, :, cols], hs.at[b, x, :, cols], left),
        ]

    def forward(u, cps):
        b, g = divmod(u, GRAN)
        cols = pl.ds(g * per * TILE, per * TILE)
        out = []
        for cp, k, part, device in zip(cps, (xm, xp), (upper, lower), (right, left)):
            cp.wait_recv()
            out.append(rcopy(hs.at[b, k, part, cols], hs.at[b, k, part, cols], device))
        return out

    far, near, passed, sent_h, fwd = {}, {}, {}, {}, {}

    def s0(u):
        far[u], near[u] = gate_up(u)

    def s1(u):
        passed[u] = pass_on(u, far[u])

    def s2(u):
        sent_h[u] = activate(u, near[u] + passed[u])

    def s3(u):
        fwd[u] = forward(u, sent_h[u])

    pieces = (((0, half),), ((0, 5 * TILE), (5 * TILE, half - 5 * TILE)))

    def down(b, into, first, lo, width):
        src = pl.ds(pl.multiple_of(first + lo, TILE), width)
        part = jnp.dot(hs[b].reshape(blk, -1), wd[:, src], preferred_element_type=F32)
        into[b, :, :, :, lo : lo + width] = part.astype(into.dtype).reshape(NZ, NY, SLAB, width)

    core, r1, r2 = {}, {}, {}

    def da(b, p):
        lo, width = pieces[b][p]
        cols = pl.ds(lo, width)
        down(b, dp, oc * half, lo, width)
        core[b, p] = rcopy(dp.at[b, :, :, :, cols], dr.at[b, :, :, :, cols], sibling)

    def db(b, p):
        down(b, own, c * half, *pieces[b][p])

    def d1(b, p):
        lo, width = pieces[b][p]
        cols = pl.ds(lo, width)
        core[b, p].wait_recv()

        def add(i, _):
            m, n = i // NY, lax.rem(i, NY)
            ds_[b, m * oc + n * c, n * oc + m * c, :, cols] = (
                own[b, m, n, :, cols] + dr[b, m, n, :, cols].astype(F32)
            ).astype(BF16)
            return 0

        lax.fori_loop(0, NZ * NY, add, 0)
        r1[b, p] = [
            rcopy(
                ds_.at[b, lax.rem(fi + i, NZ), :, :, cols], az.at[b, i - 1, :, :, cols],
                gather_second[i - 1],
            )
            for i in range(1, NZ)
        ]

    def d2(b, p):
        lo, width = pieces[b][p]
        cols = pl.ds(lo, width)
        arrive(r1[b, p])

        def add(i, _):
            total = ds_[b, fi, i, :, cols].astype(F32)
            for k in range(NZ - 1):
                total += az[b, k, i, :, cols].astype(F32)
            tt[b, i, :, cols] = total.astype(BF16)
            return 0

        lax.fori_loop(0, NY, add, 0)
        r2[b, p] = [
            rcopy(
                tt.at[b, lax.rem(si + i, NY), :, cols], tr.at[b, i - 1, :, cols],
                gather_first[i - 1],
            )
            for i in range(1, NY)
        ]

    ffn_base = recvs(7)

    def d3(b):
        for p in range(len(pieces[b])):
            arrive(r2[b, p])
        total = tt[b, si].astype(F32)
        for k in range(NY - 1):
            total += tr[b, k].astype(F32)
        for j in range(NX):
            fx[b, j] = total[4 * j : 4 * j + 4]
        for i in range(1, NX):
            to = lax.rem(x + i, NX)
            rcopy(fx.at[b, to], fr.at[c, x], at(z, y, b, to), ffn_base + c * 3 + i - 1)
        sidx = send_count[0]
        send_count[0] += 1

        def across(do):
            @pl.when(c != b)
            def _():
                do(describe(fx.at[b, x], fr.at[c, x], sibling, sidx, ffn_base + 6))

        across(lambda cp: cp.start())
        finals.append(lambda: across(lambda cp: cp.wait_send()))

        @pl.when(c == b)
        def _():
            fr[c, x] = fx[b, x]

    def kv_start():
        xwin = xa[:, :, :, :, pl.ds(pl.multiple_of(start, TILE), 2 * TILE)]
        xwin = xwin.reshape(NC * blk, 2 * TILE)
        for h in range(NC):
            kp[h] = jnp.dot(
                xwin, wpad[:, h * HD : (h + 1) * HD], preferred_element_type=F32
            ).reshape(kp.shape[1:])
        return rcopy(kp.at[oc], kr, sibling)

    def kv_first():
        kv_core.wait_recv()

        def add(i, _):
            p, q = i // NY, lax.rem(i, NY)
            for b in range(NC):
                ks[p * oc + q * c, b, q * oc + p * c] = kp[c, b, p, q] + kr[b, p, q]
            return 0

        lax.fori_loop(0, NZ * NY, add, 0)
        return [
            rcopy(ks.at[lax.rem(fi + i, NZ)], kz.at[i - 1], gather_second[i - 1])
            for i in range(1, NZ)
        ]

    def kv_second():
        arrive(kv1)
        for j in range(NY):
            kt[j] = ks[fi, :, j] + kz[0, :, j] + kz[1, :, j] + kz[2, :, j]
        return [
            rcopy(kt.at[lax.rem(si + i, NY)], ktr.at[i - 1], gather_first[i - 1])
            for i in range(1, NY)
        ]

    def kv_third():
        arrive(kv2)
        kv_sum = kt[si] + ktr[0] + ktr[1] + ktr[2]
        for b in range(NC):
            for j in range(NX):
                kx[b, j] = kv_sum[b, 4 * j : 4 * j + 4]
        return spread(kx, kxr)

    def merge():
        arrive(kv3)
        key_sum, value_sum = kxr[0, 0], kxr[1, 0]
        for j in range(1, NX):
            key_sum, value_sum = key_sum + kxr[0, j], value_sum + kxr[1, j]
        key_sum, value_sum = (v.astype(BF16).astype(F32) for v in (key_sum, value_sum))
        for r in range(4):
            key_new, value_new = key_sum[r : r + 1], value_sum[r : r + 1]
            s_new = jnp.sum(q_s[r] * key_new, axis=-1, keepdims=True) * scale
            m_old = m_s[r][:, :1]
            m = jnp.maximum(m_old, s_new)
            keep, mine = jnp.exp(m_old - m), jnp.exp(s_new - m)
            total = l_s[r][:, :1] * keep + mine
            prob = (mine / total).astype(BF16).astype(F32)
            c_s[r] = acc_s[r] * (keep / total) + prob * value_new

    def gather_heads(h, _):
        row = jnp.concatenate([c_s[r, pl.ds(h, 1), :] for r in range(4)], axis=0)
        ctx_ref[:, pl.ds(pl.multiple_of(h * HD, HD), HD)] = row
        return 0

    s0(0)
    s0(1)
    s0(2)
    g2[1]()
    sib1 = gather3(1)
    s1(1)
    s1(0)
    sib1.wait_recv()
    kv_core = kv_start()
    s0(3)
    s1(2)
    s2(0)
    kv1 = kv_first()
    s0(4)
    s2(1)
    s2(2)
    s0(5)
    s1(4)
    s1(3)
    s1(5)
    s3(0)
    s3(2)
    s3(1)
    s2(3)
    kv2 = kv_second()
    s2(5)
    s2(4)
    wdcp.wait()
    arrive(fwd[0] + fwd[1] + fwd[2])
    da(0, 0)
    s3(3)
    s3(5)
    s3(4)
    kv3 = kv_third()
    db(0, 0)
    d1(0, 0)
    arrive(fwd[3] + fwd[4] + fwd[5])
    da(1, 1)
    db(1, 1)
    da(1, 0)
    db(1, 0)
    d1(1, 1)
    d1(1, 0)
    merge()
    lax.fori_loop(0, HEADS, gather_heads, 0)
    d2(0, 0)
    d2(1, 1)
    d2(1, 0)
    d3(0)
    d3(1)
    for h in range(NC):
        for i in range(1, NX):
            describe(
                fx.at[0, 0], fr.at[h, lax.rem(x + NX - i, NX)], sibling, 0, ffn_base + h * 3 + i - 1
            ).wait_recv()
    describe(fx.at[0, 0], fr.at[oc, x], sibling, 0, ffn_base + 6).wait_recv()
    for j in range(NX):
        for h in range(NC):
            ffn_ref[:, pl.ds(j * d_dev + h * half, half)] = fr[h, j]
    for wait in finals:
        wait()


def body(tokens, gain, w_gate, w_up, w_down, w_kv, queries, key_cache, value_cache, lengths):
    batch, width = tokens.shape
    d_dev, hid = w_gate.shape
    half = d_dev // 2
    span = key_cache.shape[1]
    n_tiles = hid // TILE
    blk = NZ * NY * SLAB
    chunk = blk // NX
    per = n_tiles // GRAN
    units = NC * GRAN
    vm = pl.BlockSpec(memory_space=pltpu.VMEM)
    hbm = pl.BlockSpec(memory_space=pltpu.HBM)
    ffn, context = pl.pallas_call(
        step_kernel,
        name="step",
        out_shape=(
            jax.ShapeDtypeStruct((batch, width), F32),
            jax.ShapeDtypeStruct((batch, HEADS * HD), F32),
        ),
        in_specs=[pl.BlockSpec(memory_space=pltpu.SMEM)] + [hbm] * 9,
        out_specs=(vm, vm),
        scratch_shapes=[
            pltpu.VMEM((batch, width), BF16),
            pltpu.VMEM((1, width), F32),
            pltpu.VMEM((batch, HEADS * HD), BF16),
            pltpu.VMEM(w_kv.shape[1:], BF16),
            pltpu.VMEM((batch, span, HD), BF16),
            pltpu.VMEM((batch, span, HD), BF16),
            pltpu.VMEM((GRAN, d_dev, per * 2 * TILE), BF16),
            pltpu.VMEM((hid, d_dev), BF16),
            pltpu.VMEM((NC, NX, 4, half), F32),
            pltpu.VMEM((NC, NX, 4, half), F32),
            pltpu.VMEM((NC, NZ, NY, SLAB, d_dev), BF16),
            pltpu.VMEM((2 * TILE, 2 * HD), BF16),
            pltpu.VMEM((NC, NC, NZ, NY, SLAB, HD), F32),
            pltpu.VMEM((NC, NZ, NY, SLAB, HD), F32),
            pltpu.VMEM((NZ, NC, NY, SLAB, HD), F32),
            pltpu.VMEM((NZ - 1, NC, NY, SLAB, HD), F32),
            pltpu.VMEM((NY, NC, SLAB, HD), F32),
            pltpu.VMEM((NY - 1, NC, SLAB, HD), F32),
            pltpu.VMEM((NC, NX, 4, HD), F32),
            pltpu.VMEM((NC, NX, 4, HD), F32),
            pltpu.VMEM((units, NX, chunk, per * 2 * TILE), BF16),
            pltpu.VMEM((units, 2, chunk // 2, per * 2 * TILE), BF16),
            pltpu.VMEM((units, 2, chunk, per * 2 * TILE), BF16),
            pltpu.VMEM((NC, NX, chunk, hid), BF16),
            pltpu.VMEM((NC, NZ, NY, SLAB, half), F32),
            pltpu.VMEM((NC, NZ, NY, SLAB, half), BF16),
            pltpu.VMEM((NC, NZ, NY, SLAB, half), BF16),
            pltpu.VMEM((NC, NZ, NY, SLAB, half), BF16),
            pltpu.VMEM((NC, NZ - 1, NY, SLAB, half), BF16),
            pltpu.VMEM((NC, NY, SLAB, half), BF16),
            pltpu.VMEM((NC, NY - 1, SLAB, half), BF16),
            pltpu.VMEM((NC, NX, 4, half), F32),
            pltpu.VMEM((NC, NX, 4, half), F32),
            pltpu.VMEM((batch, HEADS, HD), F32),
            pltpu.VMEM((batch, HEADS, HD), F32),
            pltpu.VMEM((batch, HEADS, 128), F32),
            pltpu.VMEM((batch, HEADS, 128), F32),
            pltpu.VMEM((batch, HEADS, HD), F32),
            pltpu.SemaphoreType.DMA((144,)),
            pltpu.SemaphoreType.DMA((144,)),
            pltpu.SemaphoreType.DMA((5, n_tiles)),
        ],
        compiler_params=pltpu.CompilerParams(
            collective_id=0, has_side_effects=True, vmem_limit_bytes=60 << 20
        ),
    )(
        lengths, tokens, gain.reshape(1, -1), queries, w_kv[0],
        w_gate, w_up, w_down, key_cache, value_cache,
    )
    mixed = (tokens.astype(F32) + ffn).astype(BF16)
    return mixed, context.astype(BF16)


def solution(mesh):
    return jax.shard_map(
        body,
        mesh=mesh,
        in_specs=(
            P(("gx", "gy"), None),
            P(),
            P("gy", "gx"),
            P("gy", "gx"),
            P("gx", "gy"),
            P("gy", "gx", None),
            P(("gx", "gy"), None),
            P(("gx", "gy"), None, None),
            P(("gx", "gy"), None, None),
            P(("gx", "gy")),
        ),
        out_specs=(P(("gx", "gy"), None), P(("gx", "gy"), None)),
        check_vma=False,
    )
```

```python
import functools
import math

import jax
import jax.numpy as jnp
from jax import lax
from jax.experimental import pallas as pl
from jax.experimental.pallas import tpu as pltpu
from jax.sharding import PartitionSpec as P

MESH = pl.DeviceIdType.MESH
HD = 256
HEADS = 48
NZ, NY, NC, NX = 4, 4, 2, 4
SLAB = 16
TILE = 128
GRAN = 3
F32 = jnp.float32
BF16 = jnp.bfloat16


def step_kernel(
    len_ref, tok_hbm, gain_hbm, q_hbm, wkv_hbm, wg_hbm, wu_hbm, wd_hbm, k_hbm, v_hbm,
    ffn_ref, ctx_ref,
    tokens_ref, gain_ref, q_ref, wkv_ref,
    kbuf, vbuf, wgu, wd, nx, xr, xa, wpad, kp, kr, ks, kz, kt, ktr, kx, kxr,
    ps, rf, rn, hs, own, dp, dr, ds_, az, tt, tr, fx, fr,
    q_s, c_s, m_s, l_s, acc_s, ssem, rsem, lsem,
):
    d_dev = xa.shape[-1]
    half = d_dev // 2
    gx = lax.axis_index("gx")
    x = lax.axis_index("gy")
    z = gx // (NY * NC)
    y = lax.rem(gx // NC, NY)
    c = lax.rem(gx, NC)
    oc = 1 - c

    def at(zz, yy, cc, xx):
        return ((zz * NY + yy) * NC + cc, xx)

    def dev(dz=0, dy=0, dx=0):
        return at(lax.rem(z + dz, NZ), lax.rem(y + dy, NY), c, lax.rem(x + dx, NX))

    sibling = at(z, y, oc, x)
    gather_first = [dev(dy=i * oc, dz=i * c) for i in range(1, NZ)]
    gather_second = [dev(dz=i * oc, dy=i * c) for i in range(1, NZ)]
    fi, si = z * oc + y * c, y * oc + z * c

    send_count, recv_count, finals = [0], [0], []

    def sends(n):
        send_count[0] += n
        return send_count[0] - n

    def recvs(n):
        recv_count[0] += n
        return recv_count[0] - n

    def describe(src, dst, device, si_, ri):
        return pltpu.make_async_remote_copy(
            src_ref=src, dst_ref=dst, send_sem=ssem.at[si_], recv_sem=rsem.at[ri],
            device_id=device, device_id_type=MESH,
        )

    def rcopy(src, dst, device, ri=None):
        i = sends(1)
        cp = describe(src, dst, device, i, recvs(1) if ri is None else ri)
        cp.start()
        finals.append(cp.wait_send)
        return cp

    def drain():
        for wait in finals:
            wait()
        finals.clear()

    def arrive(cps):
        for cp in cps:
            cp.wait_recv()

    bar = pltpu.get_barrier_semaphore()
    peers = (
        [dev(dz=i) for i in range(1, NZ)] + [dev(dy=i) for i in range(1, NY)]
        + [at(z, y, h, lax.rem(x + i, NX)) for i in range(1, NX) for h in range(NC)] + [sibling]
    )
    for peer in peers:
        pl.semaphore_signal(bar, inc=1, device_id=peer, device_id_type=MESH)

    small = [
        pltpu.make_async_copy(src, dst, lsem.at[4, 1 + i]) for i, (src, dst) in enumerate(
            ((tok_hbm, tokens_ref), (gain_hbm, gain_ref), (q_hbm, q_ref), (wkv_hbm, wkv_ref))
        )
    ]
    kcp = [pltpu.make_async_copy(k_hbm.at[r], kbuf.at[r], lsem.at[0, r]) for r in range(4)]
    vcp = [pltpu.make_async_copy(v_hbm.at[r], vbuf.at[r], lsem.at[1, r]) for r in range(4)]
    per = wgu.shape[2] // (2 * TILE)
    n_tiles = per * GRAN

    def weight_copies(t):
        cols = pl.ds(t * TILE, TILE)
        g, lo = t // per, t % per * 2 * TILE
        return (
            pltpu.make_async_copy(wg_hbm.at[:, cols], wgu.at[g, :, pl.ds(lo, TILE)], lsem.at[2, t]),
            pltpu.make_async_copy(
                wu_hbm.at[:, cols], wgu.at[g, :, pl.ds(lo + TILE, TILE)], lsem.at[3, t]
            ),
        )

    for cp in small:
        cp.start()
    for r in range(4):
        kcp[r].start()
        vcp[r].start()
    for t in range(n_tiles):
        for cp in weight_copies(t):
            cp.start()
    wdcp = pltpu.make_async_copy(wd_hbm, wd, lsem.at[4, 0])
    wdcp.start()

    small[0].wait()
    small[1].wait()
    values = tokens_ref[...].astype(F32)
    centred = values - jnp.mean(values, axis=-1, keepdims=True)
    spread_of = jnp.mean(centred * centred, axis=-1, keepdims=True)
    normed = centred * lax.rsqrt(spread_of + 1e-05) * gain_ref[...]
    for j in range(NX):
        for h in range(NC):
            lo = j * d_dev + h * half
            nx[h, j] = normed[:, lo : lo + half]

    pl.semaphore_wait(bar, len(peers))

    def spread(src, dst):
        base = recvs(7)
        for h in range(NC):
            for i in range(1, NX):
                to = lax.rem(x + i, NX)
                rcopy(src.at[h, to], dst.at[c, x], at(z, y, h, to), base + c * 3 + i - 1)
        rcopy(src.at[oc, x], dst.at[c, x], sibling, base + 6)
        dst[c, x] = src[c, x]
        out = [
            describe(src.at[0, 0], dst.at[h, lax.rem(x + NX - i, NX)], sibling, 0, base + h * 3 + i - 1)
            for h in range(NC) for i in range(1, NX)
        ]
        return out + [describe(src.at[0, 0], dst.at[oc, x], sibling, 0, base + 6)]

    cps = spread(nx, xr)
    c0, c1 = pl.ds(0, half), pl.ds(half, half)
    ch = pl.ds(pl.multiple_of(c * half, TILE), half)
    arrive(cps)

    def gather1(b):
        xa[b, z, y, :, ch] = jnp.concatenate([xr[b, j] for j in range(NX)], axis=0).astype(BF16)
        return [
            rcopy(xa.at[b, z, y, :, ch], xa.at[b, z, y, :, ch], gather_first[i]) for i in range(NZ - 1)
        ]

    def gather2(b):
        sbase, rbase = sends(2 * NZ - 1), recvs(2 * NZ - 1)

        def group(core, i):
            if core == 0:
                return xa.at[b, lax.rem(z + NZ - i, NZ), :, :, c0]
            return xa.at[b, :, lax.rem(y + NY - i, NY), :, c1]

        def each(do):
            for core in range(NC):
                @pl.when(c == core)
                def _():
                    do(core)

        def out(core, i):
            ref = group(core, 0)
            return describe(ref, ref, gather_second[i - 1], sbase + i, rbase + i)

        def over(core, i):
            ref = group(core, i)
            k = i + NZ - 1 if i else 0
            return describe(ref, ref, sibling, sbase + k, rbase + k)

        def begin(core):
            for i in range(1, NZ):
                out(core, i).start()
            over(core, 0).start()

        def onward(core):
            for i in (1, 3, 2):
                out(core, i).wait_recv()
                over(core, i).start()

        def received(core):
            for i in range(NZ):
                over(1 - core, i).wait_recv()

        def sent(core):
            for i in range(1, NZ):
                out(core, i).wait_send()
            for i in range(NZ):
                over(core, i).wait_send()

        each(begin)
        finals.append(lambda: each(sent))
        return lambda: each(onward), lambda: each(received)

    g1 = [gather1(b) for b in range(NC)]
    scale = 1.0 / math.sqrt(HD)

    def spread_heads(h, _):
        row = q_ref[:, pl.ds(pl.multiple_of(h * HD, HD), HD)].astype(F32)
        for r in range(4):
            q_s[r, pl.ds(h, 1), :] = row[r : r + 1]
        return 0

    def attend(r):
        kcp[r].wait()
        vcp[r].wait()
        s = lax.dot_general(
            q_s[r].astype(BF16), kbuf[r], (((1,), (1,)), ((), ())), preferred_element_type=F32
        ) * scale
        live = lax.broadcasted_iota(jnp.int32, s.shape, 1) < len_ref[r]
        s = jnp.where(live, s, -jnp.inf)
        m = jnp.max(s, axis=-1, keepdims=True)
        p = jnp.exp(s - m)
        l = jnp.sum(p, axis=-1, keepdims=True)
        m_s[r] = jnp.broadcast_to(m, m_s.shape[1:])
        l_s[r] = jnp.broadcast_to(l, l_s.shape[1:])
        acc_s[r] = jnp.dot(p.astype(BF16), vbuf[r], preferred_element_type=F32)

    small[2].wait()
    lax.fori_loop(0, HEADS, spread_heads, 0)
    attend(0)
    attend(1)
    arrive(g1[0])
    g2 = [gather2(0)]
    arrive(g1[1])
    g2.append(gather2(1))
    attend(2)
    attend(3)

    small[3].wait()
    span = wkv_ref.shape[0]
    offset = gx * span
    start = jnp.minimum(offset // TILE, d_dev // TILE - 2) * TILE
    wide = jnp.concatenate(
        [wkv_ref[...].astype(F32), jnp.zeros((2 * TILE - span, 2 * HD), F32)], axis=0
    )
    wpad[...] = pltpu.roll(wide, offset - start, axis=0).astype(BF16)

    g2[0][0]()
    g2[0][1]()

    blk = NZ * NY * SLAB

    chunk = blk // NX
    part_rows = chunk // 2
    upper, lower = pl.ds(0, part_rows), pl.ds(part_rows, part_rows)
    right, left = dev(dx=1), dev(dx=NX - 1)
    xp, xm, xf = lax.rem(x + 1, NX), lax.rem(x + NX - 1, NX), lax.rem(x + 2, NX)

    def gate_up(u):
        b, g = divmod(u, GRAN)

        if b == 0:
            for t in range(per):
                for cp in weight_copies(g * per + t):
                    cp.wait()
        part = jnp.dot(xa[b].reshape(blk, d_dev), wgu[g], preferred_element_type=F32)
        for k in range(NX):
            ps[u, k] = part[k * chunk : (k + 1) * chunk].astype(BF16)
        far = [
            rcopy(ps.at[u, xf, upper], rf.at[u, 0], right),
            rcopy(ps.at[u, xf, lower], rf.at[u, 1], left),
        ]
        near = [
            rcopy(ps.at[u, xp, lower], rn.at[u, 0, lower], right),
            rcopy(ps.at[u, xm, upper], rn.at[u, 1, upper], left),
        ]
        return far, near

    def pass_on(u, far):
        out = []
        for i, (k, part, device) in enumerate(((xp, upper, right), (xm, lower, left))):
            far[i].wait_recv()
            ps[u, k, part] = (ps[u, k, part].astype(F32) + rf[u, i].astype(F32)).astype(BF16)
            out.append(rcopy(ps.at[u, k, part], rn.at[u, i, part], device))
        return out

    def activate(u, cps):
        b, g = divmod(u, GRAN)
        arrive(cps)
        for t in range(per):
            col = pl.ds(t * 2 * TILE, 2 * TILE)
            total = ps[u, x, :, col].astype(F32)
            for i in range(2):
                total += rn[u, i, :, col].astype(F32)
            gate, up = total[:, :TILE], total[:, TILE:]
            hs[b, x, :, pl.ds((g * per + t) * TILE, TILE)] = (
                gate / (1.0 + jnp.exp(-gate)) * up
            ).astype(BF16)
        cols = pl.ds(g * per * TILE, per * TILE)
        return [
            rcopy(hs.at[b, x, :, cols], hs.at[b, x, :, cols], right),
            rcopy(hs.at[b, x, :, cols], hs.at[b, x, :, cols], left),
        ]

    def forward(u, cps):
        b, g = divmod(u, GRAN)
        cols = pl.ds(g * per * TILE, per * TILE)
        out = []
        for cp, k, part, device in zip(cps, (xm, xp), (upper, lower), (right, left)):
            cp.wait_recv()
            out.append(rcopy(hs.at[b, k, part, cols], hs.at[b, k, part, cols], device))
        return out

    far, near, passed, sent_h, fwd = {}, {}, {}, {}, {}

    def s0(u):
        far[u], near[u] = gate_up(u)

    def s1(u):
        passed[u] = pass_on(u, far[u])

    def s2(u):
        sent_h[u] = activate(u, near[u] + passed[u])

    def s3(u):
        fwd[u] = forward(u, sent_h[u])

    pieces = (((0, half),), ((0, 5 * TILE), (5 * TILE, half - 5 * TILE)))

    def down(b, into, first, lo, width):
        src = pl.ds(pl.multiple_of(first + lo, TILE), width)
        part = jnp.dot(hs[b].reshape(blk, -1), wd[:, src], preferred_element_type=F32)
        into[b, :, :, :, lo : lo + width] = part.astype(into.dtype).reshape(NZ, NY, SLAB, width)

    core, r1, r2 = {}, {}, {}

    def da(b, p):
        lo, width = pieces[b][p]
        cols = pl.ds(lo, width)
        down(b, dp, oc * half, lo, width)
        core[b, p] = rcopy(dp.at[b, :, :, :, cols], dr.at[b, :, :, :, cols], sibling)

    def db(b, p):
        down(b, own, c * half, *pieces[b][p])

    def d1(b, p):
        lo, width = pieces[b][p]
        cols = pl.ds(lo, width)
        core[b, p].wait_recv()

        def add(i, _):
            m, n = i // NY, lax.rem(i, NY)
            ds_[b, m * oc + n * c, n * oc + m * c, :, cols] = (
                own[b, m, n, :, cols] + dr[b, m, n, :, cols].astype(F32)
            ).astype(BF16)
            return 0

        lax.fori_loop(0, NZ * NY, add, 0)
        r1[b, p] = [
            rcopy(
                ds_.at[b, lax.rem(fi + i, NZ), :, :, cols], az.at[b, i - 1, :, :, cols],
                gather_second[i - 1],
            )
            for i in range(1, NZ)
        ]

    def d2(b, p):
        lo, width = pieces[b][p]
        cols = pl.ds(lo, width)
        arrive(r1[b, p])

        def add(i, _):
            total = ds_[b, fi, i, :, cols].astype(F32)
            for k in range(NZ - 1):
                total += az[b, k, i, :, cols].astype(F32)
            tt[b, i, :, cols] = total.astype(BF16)
            return 0

        lax.fori_loop(0, NY, add, 0)
        r2[b, p] = [
            rcopy(
                tt.at[b, lax.rem(si + i, NY), :, cols], tr.at[b, i - 1, :, cols],
                gather_first[i - 1],
            )
            for i in range(1, NY)
        ]

    ffn_base = recvs(7)

    def d3(b):
        for p in range(len(pieces[b])):
            arrive(r2[b, p])
        total = tt[b, si].astype(F32)
        for k in range(NY - 1):
            total += tr[b, k].astype(F32)
        for j in range(NX):
            fx[b, j] = total[4 * j : 4 * j + 4]
        for i in range(1, NX):
            to = lax.rem(x + i, NX)
            rcopy(fx.at[b, to], fr.at[c, x], at(z, y, b, to), ffn_base + c * 3 + i - 1)
        sidx = sends(1)

        def across(do):
            @pl.when(c != b)
            def _():
                do(describe(fx.at[b, x], fr.at[c, x], sibling, sidx, ffn_base + 6))

        across(lambda cp: cp.start())
        finals.append(lambda: across(lambda cp: cp.wait_send()))

        @pl.when(c == b)
        def _():
            fr[c, x] = fx[b, x]

    def kv_start():
        xwin = xa[:, :, :, :, pl.ds(pl.multiple_of(start, TILE), 2 * TILE)]
        xwin = xwin.reshape(NC * blk, 2 * TILE)
        for h in range(NC):
            kp[h] = jnp.dot(
                xwin, wpad[:, h * HD : (h + 1) * HD], preferred_element_type=F32
            ).reshape(kp.shape[1:])
        return rcopy(kp.at[oc], kr, sibling)

    def kv_first():
        kv_core.wait_recv()

        def add(i, _):
            p, q = i // NY, lax.rem(i, NY)
            for b in range(NC):
                ks[p * oc + q * c, b, q * oc + p * c] = kp[c, b, p, q] + kr[b, p, q]
            return 0

        lax.fori_loop(0, NZ * NY, add, 0)
        return [
            rcopy(ks.at[lax.rem(fi + i, NZ)], kz.at[i - 1], gather_second[i - 1])
            for i in range(1, NZ)
        ]

    def kv_second():
        arrive(kv1)
        for j in range(NY):
            kt[j] = ks[fi, :, j] + kz[0, :, j] + kz[1, :, j] + kz[2, :, j]
        return [
            rcopy(kt.at[lax.rem(si + i, NY)], ktr.at[i - 1], gather_first[i - 1])
            for i in range(1, NY)
        ]

    def kv_third():
        arrive(kv2)
        kv_sum = kt[si] + ktr[0] + ktr[1] + ktr[2]
        for b in range(NC):
            for j in range(NX):
                kx[b, j] = kv_sum[b, 4 * j : 4 * j + 4]
        return spread(kx, kxr)

    def merge():
        arrive(kv3)
        key_sum, value_sum = kxr[0, 0], kxr[1, 0]
        for j in range(1, NX):
            key_sum, value_sum = key_sum + kxr[0, j], value_sum + kxr[1, j]
        key_sum, value_sum = (v.astype(BF16).astype(F32) for v in (key_sum, value_sum))
        for r in range(4):
            key_new, value_new = key_sum[r : r + 1], value_sum[r : r + 1]
            s_new = jnp.sum(q_s[r] * key_new, axis=-1, keepdims=True) * scale
            m_old = m_s[r][:, :1]
            m = jnp.maximum(m_old, s_new)
            keep, mine = jnp.exp(m_old - m), jnp.exp(s_new - m)
            total = l_s[r][:, :1] * keep + mine
            prob = (mine / total).astype(BF16).astype(F32)
            c_s[r] = acc_s[r] * (keep / total) + prob * value_new

    def gather_heads(h, _):
        row = jnp.concatenate([c_s[r, pl.ds(h, 1), :] for r in range(4)], axis=0)
        ctx_ref[:, pl.ds(pl.multiple_of(h * HD, HD), HD)] = row
        return 0

    s0(0)
    s0(1)
    s0(2)
    g2[1][0]()
    s1(1)
    s1(0)
    g2[1][1]()
    kv_core = kv_start()
    s0(3)
    s1(2)
    s2(0)
    kv1 = kv_first()
    s0(4)
    s2(1)
    s2(2)
    s0(5)
    s1(4)
    s1(3)
    s1(5)
    s3(0)
    s3(2)
    s3(1)
    s2(3)
    kv2 = kv_second()
    s2(5)
    s2(4)
    wdcp.wait()
    arrive(fwd[0] + fwd[1] + fwd[2])
    da(0, 0)
    s3(3)
    s3(5)
    s3(4)
    kv3 = kv_third()
    db(0, 0)
    d1(0, 0)
    arrive(fwd[3] + fwd[4] + fwd[5])
    da(1, 1)
    db(1, 1)
    da(1, 0)
    db(1, 0)
    d1(1, 1)
    d1(1, 0)
    merge()
    lax.fori_loop(0, HEADS, gather_heads, 0)
    drain()
    d2(0, 0)
    d2(1, 1)
    d2(1, 0)
    d3(0)
    d3(1)
    for h in range(NC):
        for i in range(1, NX):
            describe(
                fx.at[0, 0], fr.at[h, lax.rem(x + NX - i, NX)], sibling, 0, ffn_base + h * 3 + i - 1
            ).wait_recv()
    describe(fx.at[0, 0], fr.at[oc, x], sibling, 0, ffn_base + 6).wait_recv()
    for j in range(NX):
        for h in range(NC):
            ffn_ref[:, pl.ds(j * d_dev + h * half, half)] = fr[h, j]
    drain()


def finish_kernel(tokens_ref, ffn_ref, context_ref, mixed_ref, ctx_ref):
    mixed_ref[...] = (tokens_ref[...].astype(F32) + ffn_ref[...]).astype(BF16)
    ctx_ref[...] = context_ref[...].astype(BF16)


def body(tokens, gain, w_gate, w_up, w_down, w_kv, queries, key_cache, value_cache, lengths):
    batch, width = tokens.shape
    d_dev, hid = w_gate.shape
    half = d_dev // 2
    span = key_cache.shape[1]
    n_tiles = hid // TILE
    blk = NZ * NY * SLAB
    chunk = blk // NX
    per = n_tiles // GRAN
    units = NC * GRAN
    vm = pl.BlockSpec(memory_space=pltpu.VMEM)
    hbm = pl.BlockSpec(memory_space=pltpu.HBM)
    ffn, context = pl.pallas_call(
        step_kernel,
        name="step",
        out_shape=(
            jax.ShapeDtypeStruct((batch, width), F32),
            jax.ShapeDtypeStruct((batch, HEADS * HD), F32),
        ),
        in_specs=[pl.BlockSpec(memory_space=pltpu.SMEM)] + [hbm] * 9,
        out_specs=(vm, vm),
        scratch_shapes=[
            pltpu.VMEM((batch, width), BF16),
            pltpu.VMEM((1, width), F32),
            pltpu.VMEM((batch, HEADS * HD), BF16),
            pltpu.VMEM(w_kv.shape[1:], BF16),
            pltpu.VMEM((batch, span, HD), BF16),
            pltpu.VMEM((batch, span, HD), BF16),
            pltpu.VMEM((GRAN, d_dev, per * 2 * TILE), BF16),
            pltpu.VMEM((hid, d_dev), BF16),
            pltpu.VMEM((NC, NX, 4, half), F32),
            pltpu.VMEM((NC, NX, 4, half), F32),
            pltpu.VMEM((NC, NZ, NY, SLAB, d_dev), BF16),
            pltpu.VMEM((2 * TILE, 2 * HD), BF16),
            pltpu.VMEM((NC, NC, NZ, NY, SLAB, HD), F32),
            pltpu.VMEM((NC, NZ, NY, SLAB, HD), F32),
            pltpu.VMEM((NZ, NC, NY, SLAB, HD), F32),
            pltpu.VMEM((NZ - 1, NC, NY, SLAB, HD), F32),
            pltpu.VMEM((NY, NC, SLAB, HD), F32),
            pltpu.VMEM((NY - 1, NC, SLAB, HD), F32),
            pltpu.VMEM((NC, NX, 4, HD), F32),
            pltpu.VMEM((NC, NX, 4, HD), F32),
            pltpu.VMEM((units, NX, chunk, per * 2 * TILE), BF16),
            pltpu.VMEM((units, 2, chunk // 2, per * 2 * TILE), BF16),
            pltpu.VMEM((units, 2, chunk, per * 2 * TILE), BF16),
            pltpu.VMEM((NC, NX, chunk, hid), BF16),
            pltpu.VMEM((NC, NZ, NY, SLAB, half), F32),
            pltpu.VMEM((NC, NZ, NY, SLAB, half), BF16),
            pltpu.VMEM((NC, NZ, NY, SLAB, half), BF16),
            pltpu.VMEM((NC, NZ, NY, SLAB, half), BF16),
            pltpu.VMEM((NC, NZ - 1, NY, SLAB, half), BF16),
            pltpu.VMEM((NC, NY, SLAB, half), BF16),
            pltpu.VMEM((NC, NY - 1, SLAB, half), BF16),
            pltpu.VMEM((NC, NX, 4, half), F32),
            pltpu.VMEM((NC, NX, 4, half), F32),
            pltpu.VMEM((batch, HEADS, HD), F32),
            pltpu.VMEM((batch, HEADS, HD), F32),
            pltpu.VMEM((batch, HEADS, 128), F32),
            pltpu.VMEM((batch, HEADS, 128), F32),
            pltpu.VMEM((batch, HEADS, HD), F32),
            pltpu.SemaphoreType.DMA((144,)),
            pltpu.SemaphoreType.DMA((144,)),
            pltpu.SemaphoreType.DMA((5, n_tiles)),
        ],
        compiler_params=pltpu.CompilerParams(
            collective_id=0, has_side_effects=True, vmem_limit_bytes=60 << 20
        ),
    )(
        lengths, tokens, gain.reshape(1, -1), queries, w_kv[0],
        w_gate, w_up, w_down, key_cache, value_cache,
    )
    return pl.pallas_call(
        finish_kernel,
        name="finish",
        out_shape=(
            jax.ShapeDtypeStruct((batch, width), BF16),
            jax.ShapeDtypeStruct((batch, HEADS * HD), BF16),
        ),
        in_specs=[vm, vm, vm],
        out_specs=(vm, vm),
    )(tokens, ffn, context)


def solution(mesh):
    return jax.shard_map(
        body,
        mesh=mesh,
        in_specs=(
            P(("gx", "gy"), None),
            P(),
            P("gy", "gx"),
            P("gy", "gx"),
            P("gx", "gy"),
            P("gy", "gx", None),
            P(("gx", "gy"), None),
            P(("gx", "gy"), None, None),
            P(("gx", "gy"), None, None),
            P(("gx", "gy")),
        ),
        out_specs=(P(("gx", "gy"), None), P(("gx", "gy"), None)),
        check_vma=False,
    )
```

```python
import functools
import math

import jax
import jax.numpy as jnp
from jax import lax
from jax.experimental import pallas as pl
from jax.experimental.pallas import tpu as pltpu
from jax.sharding import PartitionSpec as P

MESH = pl.DeviceIdType.MESH
HD = 256
HEADS = 48
NZ, NY, NC, NX = 4, 4, 2, 4
SLAB = 16
TILE = 128
GRAN = 3
F32 = jnp.float32
BF16 = jnp.bfloat16


def step_kernel(
    len_ref, tok_hbm, gain_hbm, q_hbm, wkv_hbm, wg_hbm, wu_hbm, wd_hbm, k_hbm, v_hbm,
    ffn_ref, ctx_ref,
    tokens_ref, gain_ref, q_ref, wkv_ref,
    kbuf, vbuf, wgu, wd, nx, xr, xa, wpad, kp, kr, ks, kz, kt, ktr, kx, kxr,
    ps, rf, rn, hs, own, dp, dr, ds_, az, tt, tr, fx, fr,
    q_s, c_s, m_s, l_s, acc_s, ssem, rsem, lsem,
):
    d_dev = xa.shape[-1]
    half = d_dev // 2
    gx = lax.axis_index("gx")
    x = lax.axis_index("gy")
    z = gx // (NY * NC)
    y = lax.rem(gx // NC, NY)
    c = lax.rem(gx, NC)
    oc = 1 - c

    def at(zz, yy, cc, xx):
        return ((zz * NY + yy) * NC + cc, xx)

    def dev(dz=0, dy=0, dx=0):
        return at(lax.rem(z + dz, NZ), lax.rem(y + dy, NY), c, lax.rem(x + dx, NX))

    sibling = at(z, y, oc, x)
    gather_first = [dev(dy=i * oc, dz=i * c) for i in range(1, NZ)]
    gather_second = [dev(dz=i * oc, dy=i * c) for i in range(1, NZ)]
    fi, si = z * oc + y * c, y * oc + z * c

    send_count, recv_count, finals = [0], [0], []

    def sends(n):
        send_count[0] += n
        return send_count[0] - n

    def recvs(n):
        recv_count[0] += n
        return recv_count[0] - n

    def describe(src, dst, device, si_, ri):
        return pltpu.make_async_remote_copy(
            src_ref=src, dst_ref=dst, send_sem=ssem.at[si_], recv_sem=rsem.at[ri],
            device_id=device, device_id_type=MESH,
        )

    def rcopy(src, dst, device, ri=None):
        i = sends(1)
        cp = describe(src, dst, device, i, recvs(1) if ri is None else ri)
        cp.start()
        finals.append(cp.wait_send)
        return cp

    def drain():
        for wait in finals:
            wait()
        finals.clear()

    def arrive(cps):
        for cp in cps:
            cp.wait_recv()

    bar = pltpu.get_barrier_semaphore()
    peers = (
        [dev(dz=i) for i in range(1, NZ)] + [dev(dy=i) for i in range(1, NY)]
        + [at(z, y, h, lax.rem(x + i, NX)) for i in range(1, NX) for h in range(NC)] + [sibling]
    )
    for peer in peers:
        pl.semaphore_signal(bar, inc=1, device_id=peer, device_id_type=MESH)

    small = [
        pltpu.make_async_copy(src, dst, lsem.at[4, 1 + i]) for i, (src, dst) in enumerate(
            ((tok_hbm, tokens_ref), (gain_hbm, gain_ref), (q_hbm, q_ref), (wkv_hbm, wkv_ref))
        )
    ]
    kcp = [pltpu.make_async_copy(k_hbm.at[r], kbuf.at[r], lsem.at[0, r]) for r in range(4)]
    vcp = [pltpu.make_async_copy(v_hbm.at[r], vbuf.at[r], lsem.at[1, r]) for r in range(4)]
    per = wgu.shape[2] // (2 * TILE)
    n_tiles = per * GRAN

    def weight_copies(t):
        cols = pl.ds(t * TILE, TILE)
        g, lo = t // per, t % per * 2 * TILE
        return (
            pltpu.make_async_copy(wg_hbm.at[:, cols], wgu.at[g, :, pl.ds(lo, TILE)], lsem.at[2, t]),
            pltpu.make_async_copy(
                wu_hbm.at[:, cols], wgu.at[g, :, pl.ds(lo + TILE, TILE)], lsem.at[3, t]
            ),
        )

    for cp in small:
        cp.start()
    for r in range(4):
        kcp[r].start()
        vcp[r].start()
    for t in range(n_tiles):
        for cp in weight_copies(t):
            cp.start()
    wdcp = pltpu.make_async_copy(wd_hbm, wd, lsem.at[4, 0])
    wdcp.start()

    small[0].wait()
    small[1].wait()
    values = tokens_ref[...].astype(F32)
    centred = values - jnp.mean(values, axis=-1, keepdims=True)
    spread_of = jnp.mean(centred * centred, axis=-1, keepdims=True)
    normed = centred * lax.rsqrt(spread_of + 1e-05) * gain_ref[...]
    for j in range(NX):
        for h in range(NC):
            lo = j * d_dev + h * half
            nx[h, j] = normed[:, lo : lo + half].astype(BF16)

    pl.semaphore_wait(bar, len(peers))

    def spread(src, dst):
        base = recvs(7)
        for h in range(NC):
            for i in range(1, NX):
                to = lax.rem(x + i, NX)
                rcopy(src.at[h, to], dst.at[c, x], at(z, y, h, to), base + c * 3 + i - 1)
        rcopy(src.at[oc, x], dst.at[c, x], sibling, base + 6)
        dst[c, x] = src[c, x]
        out = [
            describe(src.at[0, 0], dst.at[h, lax.rem(x + NX - i, NX)], sibling, 0, base + h * 3 + i - 1)
            for h in range(NC) for i in range(1, NX)
        ]
        return out + [describe(src.at[0, 0], dst.at[oc, x], sibling, 0, base + 6)]

    cps = spread(nx, xr)
    c0, c1 = pl.ds(0, half), pl.ds(half, half)
    ch = pl.ds(pl.multiple_of(c * half, TILE), half)
    arrive(cps)

    def gather1(b):
        xa[b, z, y, :, ch] = jnp.concatenate(
            [xr[b, j].astype(F32) for j in range(NX)], axis=0
        ).astype(BF16)
        return [
            rcopy(xa.at[b, z, y, :, ch], xa.at[b, z, y, :, ch], gather_first[i]) for i in range(NZ - 1)
        ]

    def gather2(b):
        sbase, rbase = sends(2 * NZ - 1), recvs(2 * NZ - 1)

        def group(core, i):
            if core == 0:
                return xa.at[b, lax.rem(z + NZ - i, NZ), :, :, c0]
            return xa.at[b, :, lax.rem(y + NY - i, NY), :, c1]

        def each(do):
            for core in range(NC):
                @pl.when(c == core)
                def _():
                    do(core)

        def out(core, i):
            ref = group(core, 0)
            return describe(ref, ref, gather_second[i - 1], sbase + i, rbase + i)

        def over(core, i):
            ref = group(core, i)
            k = i + NZ - 1 if i else 0
            return describe(ref, ref, sibling, sbase + k, rbase + k)

        def begin(core):
            for i in range(1, NZ):
                out(core, i).start()
            over(core, 0).start()

        def onward(core):
            for i in (1, 3, 2):
                out(core, i).wait_recv()
                over(core, i).start()

        def received(core):
            for i in range(NZ):
                over(1 - core, i).wait_recv()

        def sent(core):
            for i in range(1, NZ):
                out(core, i).wait_send()
            for i in range(NZ):
                over(core, i).wait_send()

        each(begin)
        finals.append(lambda: each(sent))
        return lambda: each(onward), lambda: each(received)

    g1 = [gather1(b) for b in range(NC)]
    scale = 1.0 / math.sqrt(HD)

    def spread_heads(h, _):
        row = q_ref[:, pl.ds(pl.multiple_of(h * HD, HD), HD)].astype(F32)
        for r in range(4):
            q_s[r, pl.ds(h, 1), :] = row[r : r + 1]
        return 0

    def attend(r):
        kcp[r].wait()
        vcp[r].wait()
        s = lax.dot_general(
            q_s[r].astype(BF16), kbuf[r], (((1,), (1,)), ((), ())), preferred_element_type=F32
        ) * scale
        live = lax.broadcasted_iota(jnp.int32, s.shape, 1) < len_ref[r]
        s = jnp.where(live, s, -jnp.inf)
        m = jnp.max(s, axis=-1, keepdims=True)
        p = jnp.exp(s - m)
        l = jnp.sum(p, axis=-1, keepdims=True)
        m_s[r] = jnp.broadcast_to(m, m_s.shape[1:])
        l_s[r] = jnp.broadcast_to(l, l_s.shape[1:])
        acc_s[r] = jnp.dot(p.astype(BF16), vbuf[r], preferred_element_type=F32)

    small[2].wait()
    lax.fori_loop(0, HEADS, spread_heads, 0)
    attend(0)
    attend(1)
    arrive(g1[0])
    g2 = [gather2(0)]
    arrive(g1[1])
    g2.append(gather2(1))
    attend(2)
    attend(3)

    small[3].wait()
    span = wkv_ref.shape[0]
    offset = gx * span
    start = jnp.minimum(offset // TILE, d_dev // TILE - 2) * TILE
    wide = jnp.concatenate(
        [wkv_ref[...].astype(F32), jnp.zeros((2 * TILE - span, 2 * HD), F32)], axis=0
    )
    wpad[...] = pltpu.roll(wide, offset - start, axis=0).astype(BF16)

    g2[0][0]()
    g2[0][1]()

    blk = NZ * NY * SLAB

    chunk = blk // NX
    part_rows = chunk // 2
    upper, lower = pl.ds(0, part_rows), pl.ds(part_rows, part_rows)
    right, left = dev(dx=1), dev(dx=NX - 1)
    xp, xm, xf = lax.rem(x + 1, NX), lax.rem(x + NX - 1, NX), lax.rem(x + 2, NX)

    def gate_up(u):
        b, g = divmod(u, GRAN)

        if b == 0:
            for t in range(per):
                for cp in weight_copies(g * per + t):
                    cp.wait()
        part = jnp.dot(xa[b].reshape(blk, d_dev), wgu[g], preferred_element_type=F32)
        for k in range(NX):
            ps[u, k] = part[k * chunk : (k + 1) * chunk].astype(BF16)
        far = [
            rcopy(ps.at[u, xf, upper], rf.at[u, 0], right),
            rcopy(ps.at[u, xf, lower], rf.at[u, 1], left),
        ]
        near = [
            rcopy(ps.at[u, xp, lower], rn.at[u, 0, lower], right),
            rcopy(ps.at[u, xm, upper], rn.at[u, 1, upper], left),
        ]
        return far, near

    def pass_on(u, far):
        out = []
        for i, (k, part, device) in enumerate(((xp, upper, right), (xm, lower, left))):
            far[i].wait_recv()
            ps[u, k, part] = (ps[u, k, part].astype(F32) + rf[u, i].astype(F32)).astype(BF16)
            out.append(rcopy(ps.at[u, k, part], rn.at[u, i, part], device))
        return out

    def activate(u, cps):
        b, g = divmod(u, GRAN)
        arrive(cps)
        for t in range(per):
            col = pl.ds(t * 2 * TILE, 2 * TILE)
            total = ps[u, x, :, col].astype(F32)
            for i in range(2):
                total += rn[u, i, :, col].astype(F32)
            gate, up = total[:, :TILE], total[:, TILE:]
            hs[b, x, :, pl.ds((g * per + t) * TILE, TILE)] = (
                gate / (1.0 + jnp.exp(-gate)) * up
            ).astype(BF16)
        cols = pl.ds(g * per * TILE, per * TILE)
        return [
            rcopy(hs.at[b, x, :, cols], hs.at[b, x, :, cols], right),
            rcopy(hs.at[b, x, :, cols], hs.at[b, x, :, cols], left),
        ]

    def forward(u, cps):
        b, g = divmod(u, GRAN)
        cols = pl.ds(g * per * TILE, per * TILE)
        out = []
        for cp, k, part, device in zip(cps, (xm, xp), (upper, lower), (right, left)):
            cp.wait_recv()
            out.append(rcopy(hs.at[b, k, part, cols], hs.at[b, k, part, cols], device))
        return out

    far, near, passed, sent_h, fwd = {}, {}, {}, {}, {}

    def s0(u):
        far[u], near[u] = gate_up(u)

    def s1(u):
        passed[u] = pass_on(u, far[u])

    def s2(u):
        sent_h[u] = activate(u, near[u] + passed[u])

    def s3(u):
        fwd[u] = forward(u, sent_h[u])

    pieces = (((0, half),), ((0, 5 * TILE), (5 * TILE, half - 5 * TILE)))

    def down(b, into, first, lo, width):
        src = pl.ds(pl.multiple_of(first + lo, TILE), width)
        part = jnp.dot(hs[b].reshape(blk, -1), wd[:, src], preferred_element_type=F32)
        into[b, :, :, :, lo : lo + width] = part.astype(into.dtype).reshape(NZ, NY, SLAB, width)

    core, r1, r2 = {}, {}, {}

    def da(b, p):
        lo, width = pieces[b][p]
        cols = pl.ds(lo, width)
        down(b, dp, oc * half, lo, width)
        core[b, p] = rcopy(dp.at[b, :, :, :, cols], dr.at[b, :, :, :, cols], sibling)

    def db(b, p):
        down(b, own, c * half, *pieces[b][p])

    def d1(b, p):
        lo, width = pieces[b][p]
        cols = pl.ds(lo, width)
        core[b, p].wait_recv()

        def add(i, _):
            m, n = i // NY, lax.rem(i, NY)
            ds_[b, m * oc + n * c, n * oc + m * c, :, cols] = (
                own[b, m, n, :, cols] + dr[b, m, n, :, cols].astype(F32)
            ).astype(BF16)
            return 0

        lax.fori_loop(0, NZ * NY, add, 0)
        r1[b, p] = [
            rcopy(
                ds_.at[b, lax.rem(fi + i, NZ), :, :, cols], az.at[b, i - 1, :, :, cols],
                gather_second[i - 1],
            )
            for i in range(1, NZ)
        ]

    def d2(b, p):
        lo, width = pieces[b][p]
        cols = pl.ds(lo, width)
        arrive(r1[b, p])

        def add(i, _):
            total = ds_[b, fi, i, :, cols].astype(F32)
            for k in range(NZ - 1):
                total += az[b, k, i, :, cols].astype(F32)
            tt[b, i, :, cols] = total.astype(BF16)
            return 0

        lax.fori_loop(0, NY, add, 0)
        r2[b, p] = [
            rcopy(
                tt.at[b, lax.rem(si + i, NY), :, cols], tr.at[b, i - 1, :, cols],
                gather_first[i - 1],
            )
            for i in range(1, NY)
        ]

    ffn_base = recvs(7)

    def d3(b):
        for p in range(len(pieces[b])):
            arrive(r2[b, p])
        total = tt[b, si].astype(F32)
        for k in range(NY - 1):
            total += tr[b, k].astype(F32)
        for j in range(NX):
            fx[b, j] = total[4 * j : 4 * j + 4]
        for i in range(1, NX):
            to = lax.rem(x + i, NX)
            rcopy(fx.at[b, to], fr.at[c, x], at(z, y, b, to), ffn_base + c * 3 + i - 1)
        sidx = sends(1)

        def across(do):
            @pl.when(c != b)
            def _():
                do(describe(fx.at[b, x], fr.at[c, x], sibling, sidx, ffn_base + 6))

        across(lambda cp: cp.start())
        finals.append(lambda: across(lambda cp: cp.wait_send()))

        @pl.when(c == b)
        def _():
            fr[c, x] = fx[b, x]

    def kv_start():
        xwin = xa[:, :, :, :, pl.ds(pl.multiple_of(start, TILE), 2 * TILE)]
        xwin = xwin.reshape(NC * blk, 2 * TILE)
        for h in range(NC):
            kp[h] = jnp.dot(
                xwin, wpad[:, h * HD : (h + 1) * HD], preferred_element_type=F32
            ).reshape(kp.shape[1:])
        return rcopy(kp.at[oc], kr, sibling)

    def kv_first():
        kv_core.wait_recv()

        def add(i, _):
            p, q = i // NY, lax.rem(i, NY)
            for b in range(NC):
                ks[p * oc + q * c, b, q * oc + p * c] = kp[c, b, p, q] + kr[b, p, q]
            return 0

        lax.fori_loop(0, NZ * NY, add, 0)
        return [
            rcopy(ks.at[lax.rem(fi + i, NZ)], kz.at[i - 1], gather_second[i - 1])
            for i in range(1, NZ)
        ]

    def kv_second():
        arrive(kv1)
        for j in range(NY):
            kt[j] = ks[fi, :, j] + kz[0, :, j] + kz[1, :, j] + kz[2, :, j]
        return [
            rcopy(kt.at[lax.rem(si + i, NY)], ktr.at[i - 1], gather_first[i - 1])
            for i in range(1, NY)
        ]

    def kv_third():
        arrive(kv2)
        kv_sum = kt[si] + ktr[0] + ktr[1] + ktr[2]
        for b in range(NC):
            for j in range(NX):
                kx[b, j] = kv_sum[b, 4 * j : 4 * j + 4]
        return spread(kx, kxr)

    def merge():
        arrive(kv3)
        key_sum, value_sum = kxr[0, 0], kxr[1, 0]
        for j in range(1, NX):
            key_sum, value_sum = key_sum + kxr[0, j], value_sum + kxr[1, j]
        key_sum, value_sum = (v.astype(BF16).astype(F32) for v in (key_sum, value_sum))
        for r in range(4):
            key_new, value_new = key_sum[r : r + 1], value_sum[r : r + 1]
            s_new = jnp.sum(q_s[r] * key_new, axis=-1, keepdims=True) * scale
            m_old = m_s[r][:, :1]
            m = jnp.maximum(m_old, s_new)
            keep, mine = jnp.exp(m_old - m), jnp.exp(s_new - m)
            total = l_s[r][:, :1] * keep + mine
            prob = (mine / total).astype(BF16).astype(F32)
            c_s[r] = acc_s[r] * (keep / total) + prob * value_new

    def gather_heads(h, _):
        row = jnp.concatenate([c_s[r, pl.ds(h, 1), :] for r in range(4)], axis=0)
        ctx_ref[:, pl.ds(pl.multiple_of(h * HD, HD), HD)] = row
        return 0

    s0(0)
    s0(1)
    s0(2)
    g2[1][0]()
    s1(1)
    s1(0)
    g2[1][1]()
    kv_core = kv_start()
    s0(3)
    s1(2)
    s2(0)
    kv1 = kv_first()
    s0(4)
    s2(1)
    s2(2)
    s0(5)
    s1(4)
    s1(3)
    s1(5)
    s3(0)
    s3(2)
    s3(1)
    s2(3)
    kv2 = kv_second()
    s2(5)
    s2(4)
    wdcp.wait()
    arrive(fwd[0] + fwd[1] + fwd[2])
    da(0, 0)
    s3(3)
    s3(5)
    s3(4)
    kv3 = kv_third()
    db(0, 0)
    d1(0, 0)
    arrive(fwd[3] + fwd[4] + fwd[5])
    da(1, 1)
    da(1, 0)
    db(1, 1)
    d1(1, 1)
    db(1, 0)
    d1(1, 0)
    merge()
    lax.fori_loop(0, HEADS, gather_heads, 0)
    drain()
    d2(0, 0)
    d2(1, 1)
    d2(1, 0)
    d3(0)
    d3(1)
    for h in range(NC):
        for i in range(1, NX):
            describe(
                fx.at[0, 0], fr.at[h, lax.rem(x + NX - i, NX)], sibling, 0, ffn_base + h * 3 + i - 1
            ).wait_recv()
    describe(fx.at[0, 0], fr.at[oc, x], sibling, 0, ffn_base + 6).wait_recv()
    for j in range(NX):
        for h in range(NC):
            ffn_ref[:, pl.ds(j * d_dev + h * half, half)] = fr[h, j]
    drain()


def finish_kernel(tokens_ref, ffn_ref, context_ref, mixed_ref, ctx_ref):
    mixed_ref[...] = (tokens_ref[...].astype(F32) + ffn_ref[...]).astype(BF16)
    ctx_ref[...] = context_ref[...].astype(BF16)


def body(tokens, gain, w_gate, w_up, w_down, w_kv, queries, key_cache, value_cache, lengths):
    batch, width = tokens.shape
    d_dev, hid = w_gate.shape
    half = d_dev // 2
    span = key_cache.shape[1]
    n_tiles = hid // TILE
    blk = NZ * NY * SLAB
    chunk = blk // NX
    per = n_tiles // GRAN
    units = NC * GRAN
    vm = pl.BlockSpec(memory_space=pltpu.VMEM)
    hbm = pl.BlockSpec(memory_space=pltpu.HBM)
    ffn, context = pl.pallas_call(
        step_kernel,
        name="step",
        out_shape=(
            jax.ShapeDtypeStruct((batch, width), F32),
            jax.ShapeDtypeStruct((batch, HEADS * HD), F32),
        ),
        in_specs=[pl.BlockSpec(memory_space=pltpu.SMEM)] + [hbm] * 9,
        out_specs=(vm, vm),
        scratch_shapes=[
            pltpu.VMEM((batch, width), BF16),
            pltpu.VMEM((1, width), F32),
            pltpu.VMEM((batch, HEADS * HD), BF16),
            pltpu.VMEM(w_kv.shape[1:], BF16),
            pltpu.VMEM((batch, span, HD), BF16),
            pltpu.VMEM((batch, span, HD), BF16),
            pltpu.VMEM((GRAN, d_dev, per * 2 * TILE), BF16),
            pltpu.VMEM((hid, d_dev), BF16),
            pltpu.VMEM((NC, NX, 4, half), BF16),
            pltpu.VMEM((NC, NX, 4, half), BF16),
            pltpu.VMEM((NC, NZ, NY, SLAB, d_dev), BF16),
            pltpu.VMEM((2 * TILE, 2 * HD), BF16),
            pltpu.VMEM((NC, NC, NZ, NY, SLAB, HD), F32),
            pltpu.VMEM((NC, NZ, NY, SLAB, HD), F32),
            pltpu.VMEM((NZ, NC, NY, SLAB, HD), F32),
            pltpu.VMEM((NZ - 1, NC, NY, SLAB, HD), F32),
            pltpu.VMEM((NY, NC, SLAB, HD), F32),
            pltpu.VMEM((NY - 1, NC, SLAB, HD), F32),
            pltpu.VMEM((NC, NX, 4, HD), F32),
            pltpu.VMEM((NC, NX, 4, HD), F32),
            pltpu.VMEM((units, NX, chunk, per * 2 * TILE), BF16),
            pltpu.VMEM((units, 2, chunk // 2, per * 2 * TILE), BF16),
            pltpu.VMEM((units, 2, chunk, per * 2 * TILE), BF16),
            pltpu.VMEM((NC, NX, chunk, hid), BF16),
            pltpu.VMEM((NC, NZ, NY, SLAB, half), F32),
            pltpu.VMEM((NC, NZ, NY, SLAB, half), BF16),
            pltpu.VMEM((NC, NZ, NY, SLAB, half), BF16),
            pltpu.VMEM((NC, NZ, NY, SLAB, half), BF16),
            pltpu.VMEM((NC, NZ - 1, NY, SLAB, half), BF16),
            pltpu.VMEM((NC, NY, SLAB, half), BF16),
            pltpu.VMEM((NC, NY - 1, SLAB, half), BF16),
            pltpu.VMEM((NC, NX, 4, half), F32),
            pltpu.VMEM((NC, NX, 4, half), F32),
            pltpu.VMEM((batch, HEADS, HD), F32),
            pltpu.VMEM((batch, HEADS, HD), F32),
            pltpu.VMEM((batch, HEADS, 128), F32),
            pltpu.VMEM((batch, HEADS, 128), F32),
            pltpu.VMEM((batch, HEADS, HD), F32),
            pltpu.SemaphoreType.DMA((144,)),
            pltpu.SemaphoreType.DMA((144,)),
            pltpu.SemaphoreType.DMA((5, n_tiles)),
        ],
        compiler_params=pltpu.CompilerParams(
            collective_id=0, has_side_effects=True, vmem_limit_bytes=60 << 20
        ),
    )(
        lengths, tokens, gain.reshape(1, -1), queries, w_kv[0],
        w_gate, w_up, w_down, key_cache, value_cache,
    )
    return pl.pallas_call(
        finish_kernel,
        name="finish",
        out_shape=(
            jax.ShapeDtypeStruct((batch, width), BF16),
            jax.ShapeDtypeStruct((batch, HEADS * HD), BF16),
        ),
        in_specs=[vm, vm, vm],
        out_specs=(vm, vm),
    )(tokens, ffn, context)


def solution(mesh):
    return jax.shard_map(
        body,
        mesh=mesh,
        in_specs=(
            P(("gx", "gy"), None),
            P(),
            P("gy", "gx"),
            P("gy", "gx"),
            P("gx", "gy"),
            P("gy", "gx", None),
            P(("gx", "gy"), None),
            P(("gx", "gy"), None, None),
            P(("gx", "gy"), None, None),
            P(("gx", "gy")),
        ),
        out_specs=(P(("gx", "gy"), None), P(("gx", "gy"), None)),
        check_vma=False,
    )
```
